256 devices in a mesh: ctx: 32 (over z, y_lo, core), tp: 8 (over x, y_hi).
Axes of the slice: x: 4, y: 4 (y_hi: 2, y_lo: 2; y = y_hi * 2 + y_lo), z: 8, core: 2. Of those that a mesh axis runs over, the one named last changes fastest.
Arguments:
- q_prompt: bfloat16 [8192, 7168], P('ctx', 'tp'), may hold values from -64 to 64
- kv_prompt: bfloat16 [8192, 8, 256], P('ctx', 'tp'), may hold values from -6 to 6
- q_ext: bfloat16 [2048, 7168], P('ctx', 'tp'), may hold values from -64 to 64
- kv_ext: bfloat16 [2048, 8, 256], P('ctx', 'tp'), may hold values from -6 to 6
- pool: bfloat16 [192, 128, 8, 256], P('ctx', None, 'tp'), may hold values from -6 to 6
- page_slot_table: int32 [144], replicated, may hold values from 0 to 191, as said below
Outputs:
- context: bfloat16 [10240, 7168], P(('ctx', 'tp'))
- pool_out: bfloat16 [192, 128, 8, 256], P('ctx', None, 'tp')
The draws below stay inside these ranges and needn't reach their ends.
Inputs may be any that keep to these rules, and one draw needn't show every extreme that they name: `page_slot_table`: distinct slot numbers, one per page: entries 0 to 63 are the old cache's pages, then the extension's 16 pages in order, then the prompt's 64 pages in order; every block of 6 slots (slots c * 6 to (c + 1) * 6 - 1) holds exactly 2 old pages.
All inputs are finite; a program needn't handle non-finite values.
Results may differ from the reference program's by a relative error of at most 0.006.
Values may be sent and summed in bfloat16 or wider, within the bound.
No kernel may reach another device: no remote copies, remote signals or barrier semaphores. Data moves between devices by JAX's collectives and lax.ppermute only.
A program may use at most 64 MiB of HBM per device.

```python
import jax
import jax.numpy as jnp
from jax import lax

QUERY_HEADS = 56
KEY_VALUE_HEADS = 8
HEAD_SIZE = 128
PAGE_TOKENS = 128
BLK = 128
EXT_DEV = 64
OLD_PER = 2
PROMPT = 8192
EXT = 2048
PRIOR_PAGES = 64
EXT_PAGES = 16
TOTAL_PAGES = 144
SLOTS_DEV = 6
POOL_SLOTS = 192
ROWS = 10240
N_CTX = 32


def key_values(key, label_name, token_count):
    return jnp.clip(jax.random.normal(jax.random.fold_in(key, label_name), (token_count, KEY_VALUE_HEADS, 2 * HEAD_SIZE), jnp.float32), -6.0, 6.0)


def drawn_queries(key, label_name, token_count):
    drawn = jax.random.normal(jax.random.fold_in(key, label_name + 1), (token_count, QUERY_HEADS * HEAD_SIZE), jnp.float32)
    return jnp.clip(drawn, -64.0, 64.0)


def draw_q_prompt(key, part):
    return drawn_queries(key, 10, PROMPT).astype(jnp.bfloat16)


def draw_kv_prompt(key, part):
    return key_values(key, 10, PROMPT).astype(jnp.bfloat16)


def draw_q_ext(key, part):
    return drawn_queries(key, 20, EXT).astype(jnp.bfloat16)


def draw_kv_ext(key, part):
    return key_values(key, 20, EXT).astype(jnp.bfloat16)


def draw_page_slot_table(key, part):
    owners = PRIOR_PAGES // OLD_PER
    owner_ids = jnp.arange(owners, dtype=jnp.int32)
    owner_keys = jax.vmap(lambda c: jax.random.fold_in(jax.random.fold_in(key, 40), c))(owner_ids)
    local = jax.vmap(lambda k: jax.random.permutation(k, SLOTS_DEV).astype(jnp.int32))(owner_keys)
    wanted = jnp.where(owner_ids == 0, 0, jnp.where(owner_ids == owners - 1, SLOTS_DEV - 1, local[:, 0]))
    shifted = (local + (wanted - local[:, 0])[:, None]) % SLOTS_DEV
    slots = (shifted + owner_ids[:, None] * SLOTS_DEV).astype(jnp.int32)
    old_slots = slots[:, :OLD_PER].reshape(PRIOR_PAGES)
    spare = slots[:, OLD_PER:].reshape(owners * (SLOTS_DEV - OLD_PER))
    old_order = jax.random.permutation(jax.random.fold_in(key, 41), PRIOR_PAGES)
    spare_order = jax.random.permutation(jax.random.fold_in(key, 42), owners * (SLOTS_DEV - OLD_PER))
    fresh = spare[spare_order][:TOTAL_PAGES - PRIOR_PAGES]
    return jnp.concatenate([old_slots[old_order], fresh]).astype(jnp.int32)


def levels(own_key, dims, split, least, largest):
    def one(axis_at, shards_of):
        heights = jax.random.uniform(jax.random.fold_in(jax.random.fold_in(own_key, 6), axis_at), (shards_of,), jnp.float32, least / len(split), largest / len(split))
        return jnp.repeat(jnp.exp(heights), dims[axis_at] // shards_of).reshape((-1,) + (1,) * (len(dims) - axis_at - 1))

    level = one(*split[0])
    for cut in split[1:]:
        level = level * one(*cut)
    return level


def normal_values(stream_key, extent, spread, bound, split=(), kind=jnp.bfloat16):
    gain = levels(stream_key, extent, split, -0.22, 0.18) if split else 1.0
    result = jax.random.normal(stream_key, extent, jnp.float32) * spread * gain
    return jnp.minimum(jnp.maximum(result, -bound), bound).astype(kind)


def setup_inputs(seed: int = 0) -> dict:
    key_of = jax.random.split(jax.random.key(seed), 7)
    return {
        "q_prompt": draw_q_prompt(jax.random.fold_in(key_of[6], 71), 0),
        "kv_prompt": draw_kv_prompt(jax.random.fold_in(key_of[6], 71), 0),
        "q_ext": draw_q_ext(jax.random.fold_in(key_of[6], 71), 0),
        "kv_ext": draw_kv_ext(jax.random.fold_in(key_of[6], 71), 0),
        "pool": normal_values(key_of[4], (POOL_SLOTS, PAGE_TOKENS, KEY_VALUE_HEADS, 2 * HEAD_SIZE), 1.0, 6.0, ((0, 32), (2, 8))),
        "page_slot_table": draw_page_slot_table(jax.random.fold_in(key_of[6], 71), 0),
    }


MASKED_SCORE = -1e30


def prompt_positions():
    rows = jnp.arange(PROMPT, dtype=jnp.int32)
    shard_index = rows // (2 * BLK)
    inner = rows % (2 * BLK)
    return jnp.where(inner < BLK, shard_index * BLK + inner, PROMPT - (shard_index + 2) * BLK + inner).astype(jnp.int32)


def attend(query_rows, query_pos, keys, values, key_pos):
    token_count = query_rows.shape[0]
    query_cluster = QUERY_HEADS // KEY_VALUE_HEADS
    width_total = 128 if token_count % 128 == 0 else token_count
    block_list = query_rows.reshape(token_count // width_total, width_total, KEY_VALUE_HEADS, query_cluster, HEAD_SIZE)
    block_pos = query_pos.reshape(token_count // width_total, width_total)
    keys_wide = keys.astype(jnp.float32)
    values_wide = values.astype(jnp.float32)

    def one_block(item):
        block_rows, rows_pos = item
        scores = jnp.einsum("qhgd,khd->hgqk", block_rows.astype(jnp.float32), keys_wide) * (HEAD_SIZE ** -0.5)
        allowed = key_pos[None, :] <= rows_pos[:, None]
        scores = jnp.where(allowed[None, None], scores, MASKED_SCORE)
        highest = jnp.max(scores, axis=-1, keepdims=True)
        weights = jnp.where(allowed[None, None], jnp.exp(scores - highest), 0.0)
        total = jnp.sum(weights, axis=-1)
        rounded = lax.optimization_barrier(weights.astype(jnp.bfloat16)).astype(jnp.float32)
        mixed = jnp.einsum("hgqk,khd->qhgd", rounded, values_wide)
        output = mixed / jnp.transpose(total, (2, 0, 1))[..., None]
        return output.astype(jnp.bfloat16).reshape(width_total, QUERY_HEADS * HEAD_SIZE)

    return lax.map(one_block, (block_list, block_pos)).reshape(token_count, QUERY_HEADS * HEAD_SIZE)


def reference(q_prompt, kv_prompt, q_ext, kv_ext, pool, page_slot_table):
    prompt_pos = prompt_positions()
    first_context = attend(q_prompt, prompt_pos, kv_prompt[..., :HEAD_SIZE], kv_prompt[..., HEAD_SIZE:], prompt_pos)
    prior_rows = pool[page_slot_table[:PRIOR_PAGES]].reshape(PRIOR_PAGES * PAGE_TOKENS, KEY_VALUE_HEADS, 2 * HEAD_SIZE)
    all_keys = jnp.concatenate([prior_rows, kv_ext], axis=0)
    tail_pos = jnp.arange(EXT, dtype=jnp.int32)
    key_pos = jnp.concatenate([jnp.full((PRIOR_PAGES * PAGE_TOKENS,), -1, jnp.int32), tail_pos])
    second_context = attend(q_ext, tail_pos, all_keys[..., :HEAD_SIZE], all_keys[..., HEAD_SIZE:], key_pos)
    joined = jnp.concatenate([first_context.reshape(N_CTX, 2 * BLK, QUERY_HEADS * HEAD_SIZE), second_context.reshape(N_CTX, EXT_DEV, QUERY_HEADS * HEAD_SIZE)], axis=1)
    context = joined.reshape(ROWS, QUERY_HEADS * HEAD_SIZE)
    slot_list = jnp.concatenate([page_slot_table[PRIOR_PAGES + tail_pos // PAGE_TOKENS], page_slot_table[PRIOR_PAGES + EXT_PAGES + prompt_pos // PAGE_TOKENS]]).astype(jnp.int32)
    offsets = jnp.concatenate([tail_pos % PAGE_TOKENS, prompt_pos % PAGE_TOKENS]).astype(jnp.int32)
    pool_out = pool.at[slot_list, offsets].set(jnp.concatenate([kv_ext, kv_prompt], axis=0))
    return context, pool_out
```

```python
import jax
import jax.numpy as jnp
from jax import lax
from jax.experimental import pallas as pl
from jax.experimental.pallas import tpu as pltpu
from jax.sharding import PartitionSpec as P

HEADS = 7
HD = 128
NEG = -1e30
C1 = 1.4426950408889634 * HD ** -0.5
F32 = jnp.float32
BF = jnp.bfloat16

VMEM = pl.BlockSpec(memory_space=pltpu.VMEM)
SMEM = pl.BlockSpec(memory_space=pltpu.SMEM)
ANY = pl.BlockSpec(memory_space=pl.ANY)


def params():
    return pltpu.CompilerParams(vmem_limit_bytes=48 << 20)


def cost(flops, elems, nbytes):
    return pl.CostEstimate(flops=int(flops), transcendentals=int(elems), bytes_accessed=int(nbytes))


def update(q_ref, q0, state, rows, chunk, blocks, fix=None):
    kv = blocks[0] if len(blocks) == 1 else jnp.concatenate(blocks, axis=0)
    keys = kv[:, :HD]
    values = jnp.concatenate([jnp.ones((kv.shape[0], HD), BF), kv[:, HD:]], axis=1)
    for r in range(0, rows, chunk):
        at = pl.ds(q0 + r, chunk)
        s = lax.dot_general(
            q_ref[at, :], keys, (((1,), (1,)), ((), ())), preferred_element_type=F32
        )
        if fix is not None:
            s = fix(s, r)
        m_old = state[at, :HD]
        m_new = jnp.maximum(m_old, jnp.max(s, axis=1, keepdims=True))
        p = jnp.exp2((s - m_new[:, :1]) * C1).astype(BF)
        alpha = jnp.exp2((m_old - m_new) * C1)
        pv = lax.dot_general(p, values, (((1,), (0,)), ((), ())), preferred_element_type=F32)
        state[at, :HD] = m_new
        state[at, HD:] = state[at, HD:] * jnp.concatenate([alpha, alpha], axis=1) + pv


def position(idx_ref):
    i = idx_ref[0]
    return i // 4, (i // 2) % 2, i % 2


def prep_body(idx_ref, table_ref, pool_ref, kvp_ref, kve_ref, x_ref, p_ref, sems):
    base = idx_ref[0] * 6

    def scan(j, found):
        n, a, b = found
        local = table_ref[j] - base
        inside = (local >= 0) & (local < 6)
        a = jnp.where(inside & (n == 0), local, a)
        b = jnp.where(inside & (n == 1), local, b)
        return n + inside.astype(jnp.int32), a, b

    zero = jnp.int32(0)
    early = [
        pltpu.make_async_copy(kvp_ref, x_ref.at[256:512], sems.at[0]),
        pltpu.make_async_copy(kve_ref, x_ref.at[512:576], sems.at[1]),
        pltpu.make_async_copy(kvp_ref, p_ref.at[0:256], sems.at[2]),
        pltpu.make_async_copy(kve_ref, p_ref.at[256:320], sems.at[3]),
    ]
    for copy in early:
        copy.start()
    _, a, b = lax.fori_loop(0, 64, scan, (zero, zero, zero))
    late = [
        pltpu.make_async_copy(pool_ref.at[a], x_ref.at[0:128], sems.at[4]),
        pltpu.make_async_copy(pool_ref.at[b], x_ref.at[128:256], sems.at[5]),
    ]
    for copy in late:
        copy.start()
    for copy in early + late:
        copy.wait()


def first_body(idx_ref, qp_ref, qe_ref, qy_ref, x_ref, xc_ref, y_ref, yc_ref, qs_ref, qx_ref, sp_ref, se_ref):
    z, y, c = position(idx_ref)
    j = 2 * y + c
    for h in range(HEADS):
        cols = slice(h * HD, (h + 1) * HD)
        qs_ref[h * 128:(h + 1) * 128, :] = qp_ref[0:128, cols]
        qs_ref[896 + h * 128:896 + (h + 1) * 128, :] = qp_ref[128:256, cols]
        qx_ref[h * 64:(h + 1) * 64, :] = qe_ref[:, cols]
        qx_ref[448 + h * 64:448 + (h + 1) * 64, :] = qy_ref[:, cols]
    for state in (sp_ref, se_ref):
        state[:, :HD] = jnp.full((state.shape[0], HD), NEG, F32)
        state[:, HD:] = jnp.zeros((state.shape[0], 2 * HD), F32)

    def shown(seen, width):
        return jnp.full((1, width), jnp.where(seen, 0.0, NEG), F32)

    rows = lax.broadcasted_iota(jnp.int32, (128, 128), 0)
    lanes = lax.broadcasted_iota(jnp.int32, (128, 128), 1)
    causal = jnp.where(rows >= lanes, 0.0, NEG).astype(F32)
    others = (j ^ 1, j ^ 2, j ^ 3)
    front = jnp.concatenate([shown(o < j, 128) for o in others], axis=1)
    back = jnp.concatenate([shown(o > j, 128) for o in others], axis=1)

    def fix_front(s, r):
        return jnp.concatenate([s[:, :128] + causal, s[:, 128:] + front], axis=1)

    def fix_back(s, r):
        return jnp.concatenate([s[:, :512], s[:, 512:640] + causal, s[:, 640:] + back], axis=1)

    firsts = [x_ref[256:384, :], xc_ref[256:384, :], y_ref[0:128, :], yc_ref[0:128, :]]
    seconds = [x_ref[384:512, :], xc_ref[384:512, :], y_ref[128:256, :], yc_ref[128:256, :]]
    update(qs_ref, 0, sp_ref, 896, 128, firsts, fix_front)
    update(qs_ref, 896, sp_ref, 896, 128, firsts + seconds, fix_back)

    tokens = lax.broadcasted_iota(jnp.int32, (448, 128), 0) % 64
    slots = lax.broadcasted_iota(jnp.int32, (448, 128), 1)
    own = jnp.where(
        slots < 64,
        jnp.where(tokens >= slots, 0.0, NEG).astype(F32),
        jnp.full((448, 128), jnp.where(c == 1, 0.0, NEG), F32),
    )
    mate = shown(y == 0, 128)

    def fix_ext(s, r):
        tail = s[:, 512:] + (own if r == 0 else mate)
        return jnp.concatenate([s[:, :512], tail], axis=1)

    update(
        qx_ref, 0, se_ref, 896, 448,
        [x_ref[0:256, :], xc_ref[0:256, :], x_ref[512:576, :], xc_ref[512:576, :]], fix_ext,
    )


def ext_plane(z, plane, qx_ref, se_ref, old, old_c, ext, ext_c):
    bias = jnp.full((1, 128), jnp.where(plane < z, 0.0, NEG), F32)

    def fix(s, r):
        return jnp.concatenate([s[:, :512], s[:, 512:] + bias], axis=1)

    update(qx_ref, 0, se_ref, 896, 448, [old, old_c, ext, ext_c], fix)


def selected(z, plane, qs_ref, sp_ref, parts):
    later = plane > z
    off = jnp.where(later, 128, 0)
    blocks = [ref[pl.ds(pl.multiple_of(row + off, 128) if row % 128 == 0 else pl.multiple_of(row + off, 64), 128), :] for ref, row in parts]
    q0 = pl.multiple_of(jnp.where(later, 896, 0), 128)
    update(qs_ref, q0, sp_ref, 896, 448, blocks)


def step_body(k, *refs):
    idx_ref, qs_ref, qx_ref = refs[:3]
    z, _, _ = position(idx_ref)
    minus = (z + 8 - k) % 8
    plus = (z + k) % 8
    now = refs[3:7]
    refs = refs[7:]
    before = None
    if k > 1:
        before, refs = refs[:4], refs[4:]
    if k == 1:
        se_in, se_ref = refs
    else:
        sp_in, se_in, sp_ref, se_ref = refs[:4]
        sp_ref[...] = sp_in[...]
    se_ref[...] = se_in[...]
    fa, fac, fb, fbc = now
    if k < 4:
        for plane, r, rc in ((minus, fa, fac), (plus, fb, fbc)):
            ext_plane(
                z, plane, qx_ref, se_ref,
                r[0:256, :], rc[0:256, :], r[512:576, :], rc[512:576, :],
            )
        ya = 576
        yb = 576
    else:
        ext_plane(z, plus, qx_ref, se_ref, fb[0:256, :], fbc[0:256, :], fa[256:320, :], fac[256:320, :])
        ya = 320
        yb = 256
    if k > 1:
        ga, gac, gb, gbc = before
        parts_a = [(ga, 256), (gac, 256), (fa, ya), (fac, ya)]
        parts_b = [(gb, 256), (gbc, 256), (fb, yb), (fbc, yb)]
        update(
            qs_ref, 896, sp_ref, 896, 128,
            [ref[row:row + 128, :] for ref, row in parts_a + parts_b],
        )
        selected(z, (z + 9 - k) % 8, qs_ref, sp_ref, parts_a)
        selected(z, (z + k - 1) % 8, qs_ref, sp_ref, parts_b)
    if k == 4:
        send_ref = refs[4]
        part = se_ref[448:896, :]
        total = part[:, HD:2 * HD]
        level = part[:, :HD] * C1 + jnp.log2(total)
        hi = level.astype(BF)
        rest = level - hi.astype(F32)
        mid = rest.astype(BF)
        low = (rest - mid.astype(F32)).astype(BF)
        lane = lax.broadcasted_iota(jnp.int32, (448, HD), 1)
        stats = jnp.where(
            lane == 0, hi.astype(F32), jnp.where(lane == 1, mid.astype(F32), low.astype(F32))
        )
        send_ref[:, :HD] = (part[:, 2 * HD:] / total).astype(BF)
        send_ref[:, HD:] = stats.astype(BF)


def last_body(idx_ref, qs_ref, g_ref, gc_ref, ra_ref, rac_ref, rb_ref, rbc_ref, sp_in, se_ref, got_ref, out_ref, sp_ref):
    z, _, _ = position(idx_ref)
    plane = (z + 4) % 8
    sp_ref[...] = sp_in[...]
    firsts = [g_ref[0:128, :], gc_ref[0:128, :], ra_ref[...], rac_ref[...]]
    update(qs_ref, 896, sp_ref, 896, 448, firsts)

    @pl.when(plane < z)
    def _():
        update(qs_ref, 0, sp_ref, 896, 448, firsts)

    @pl.when(plane > z)
    def _():
        seconds = [g_ref[128:256, :], gc_ref[128:256, :], rb_ref[0:128, :], rbc_ref[0:128, :]]
        update(qs_ref, 896, sp_ref, 896, 448, seconds)

    for b in range(2):
        for h in range(HEADS):
            at = slice(b * 896 + h * 128, b * 896 + (h + 1) * 128)
            out_ref[b * 128:(b + 1) * 128, h * HD:(h + 1) * HD] = (
                sp_ref[at, 2 * HD:] / sp_ref[at, HD:2 * HD]
            ).astype(BF)
    for h in range(HEADS):
        at = slice(h * 64, (h + 1) * 64)
        total = se_ref[at, HD:2 * HD]
        level = se_ref[at, :HD] * C1 + jnp.log2(total)
        mine = se_ref[at, 2 * HD:] / total
        got = got_ref[at, :].astype(F32)
        level_y = got[:, HD:HD + 1] + got[:, HD + 1:HD + 2] + got[:, HD + 2:HD + 3]
        top = jnp.maximum(level, level_y)
        wa = jnp.exp2(level - top)
        wb = jnp.exp2(level_y - top)
        out_ref[256:320, h * HD:(h + 1) * HD] = (
            (wa * mine + wb * got[:, :HD]) / (wa + wb)
        ).astype(BF)


def pages_body(idx_ref, table_ref, pool_ref, *refs):
    srcs, out_ref, slot_of, sems = refs[:24], refs[24], refs[25], refs[26]
    z, y, c = position(idx_ref)
    base = idx_ref[0] * 6
    for i in range(6):
        slot_of[i] = jnp.int32(-1)

    def scan(t, carry):
        local = table_ref[t] - base

        @pl.when((local >= 0) & (local < 6))
        def _():
            slot_of[local] = t

        return carry

    lax.fori_loop(64, 144, scan, 0)
    steps = {k: srcs[4 * k:4 * k + 4] for k in range(6)}

    def each(i, carry):
        t = slot_of[i]

        def put(src, row, count, to):
            pltpu.make_async_copy(
                src.at[pl.ds(row, count)], out_ref.at[i, pl.ds(to, count)], sems.at[i]
            ).start()

        @pl.when(t < 0)
        def _():
            pltpu.make_async_copy(pool_ref.at[i], out_ref.at[i], sems.at[i]).start()

        def from_shard(s, go, kind):
            dz = (s // 4 + 8 - z) % 8
            dy = (s // 2) % 2 != y
            dc = s % 2 != c
            cc = s % 2
            for mate in range(2):
                on = go & (dc if mate else jnp.logical_not(dc))
                table = [(0, False, steps[0][mate], 256), (0, True, steps[0][2 + mate], 0)]
                for k in (1, 2, 3):
                    table.append((8 - k, False, steps[k][mate], 256))
                    table.append((k, False, steps[k][2 + mate], 256))
                for k in (2, 3):
                    table.append((9 - k, True, steps[k][mate], 576))
                    table.append((k - 1, True, steps[k][2 + mate], 576))
                table.append((4, False, steps[4][mate], 0))
                table.append((5, True, steps[4][mate], 320))
                table.append((3, True, steps[4][2 + mate], 256))
                if kind == 0:
                    table.append((4, True, steps[5][mate], 0))
                else:
                    table.append((4, True, steps[5][2 + mate], -128))
                for d, other, ref, row in table:
                    @pl.when(on & (dz == d) & (dy if other else jnp.logical_not(dy)))
                    def _(ref=ref, row=row):
                        if kind == 2:
                            put(ref, row + 256, 64, pl.multiple_of(cc * 64, 64))
                        else:
                            put(ref, row + 128 * kind, 128, 0)

        e = t - 64
        is_ext = (t >= 64) & (t < 80)
        from_shard(2 * e, is_ext, 2)
        from_shard(2 * e + 1, is_ext, 2)
        p = t - 80
        from_shard(p, (t >= 80) & (p < 32), 0)
        from_shard(63 - p, (t >= 80) & (p >= 32), 1)
        return carry

    lax.fori_loop(0, 6, each, 0)

    def wait(i, carry):
        pltpu.make_async_copy(pool_ref.at[i], out_ref.at[i], sems.at[i]).wait()
        return carry

    lax.fori_loop(0, 6, wait, 0)


def body(q_prompt, kv_prompt, q_ext, kv_ext, pool, page_slot_table):
    idx = lax.axis_index("ctx").astype(jnp.int32).reshape(1)
    kvp = kv_prompt.reshape(256, 256)
    kve = kv_ext.reshape(64, 256)
    pages = pool.reshape(6, 128, 256)

    def shift(x, d):
        return lax.ppermute(x, "ctx", [(i, (i + 4 * d) % 32) for i in range(32)])

    def flip_y(x):
        return lax.ppermute(x, "ctx", [(i, i ^ 2) for i in range(32)])

    def flip_c(x):
        return lax.ppermute(x, "ctx", [(i, i ^ 1) for i in range(32)])

    def arr(shape, dtype=BF):
        return jax.ShapeDtypeStruct(shape, dtype)

    x, p = pl.pallas_call(
        prep_body,
        out_shape=(arr((576, 256)), arr((320, 256))),
        in_specs=[SMEM, SMEM, ANY, ANY, ANY],
        out_specs=(ANY, ANY),
        scratch_shapes=[pltpu.SemaphoreType.DMA((6,))],
        compiler_params=params(),
        name="prep",
    )(idx, page_slot_table, pages, kvp, kve)

    yp = flip_y(p)
    a1, b1 = shift(x, 1), shift(x, -1)
    qy = flip_y(q_ext)
    xc, yc = flip_c(x), flip_c(yp)

    sp_t, se_t = arr((1792, 384), F32), arr((896, 384), F32)
    qs, qx, sp, se = pl.pallas_call(
        first_body,
        out_shape=(arr((1792, 128)), arr((896, 128)), sp_t, se_t),
        in_specs=[SMEM] + [VMEM] * 7,
        out_specs=(VMEM,) * 4,
        compiler_params=params(),
        cost_estimate=cost(2e9, 2e6, 4e6),
        name="own_plane",
    )(idx, q_prompt, q_ext, qy, x, xc, yp, yc)

    def step(k, now, before, sp, se):
        outs = (sp_t, se_t) if k > 1 else (se_t,)
        if k == 4:
            outs = outs + (arr((448, 256)),)
        args = [idx, qs, qx, *now, *(before or ()), *((sp, se) if k > 1 else (se,))]
        n = len(args)
        alias = {n - 2: 0, n - 1: 1} if k > 1 else {n - 1: 0}
        return pl.pallas_call(
            lambda *refs: step_body(k, *refs),
            out_shape=outs,
            in_specs=[SMEM] + [VMEM] * (n - 1),
            out_specs=(VMEM,) * len(outs),
            input_output_aliases=alias,
            compiler_params=params(),
            cost_estimate=cost(2e9 if k > 1 else 6e8, 3e6 if k > 1 else 1.2e6, 8e6),
            name=f"step{k}",
        )(*args)

    n1 = (a1, flip_c(a1), b1, flip_c(b1))
    a2 = shift(jnp.concatenate([a1, yp], axis=0), 1)
    b2 = shift(jnp.concatenate([b1, yp], axis=0), -1)
    (se,) = step(1, n1, None, None, se)
    n2 = (a2, flip_c(a2), b2, flip_c(b2))
    a3, b3 = shift(a2, 1), shift(b2, -1)
    sp, se = step(2, n2, n1, sp, se)
    n3 = (a3, flip_c(a3), b3, flip_c(b3))
    a4 = shift(a3[256:896], 1)
    b4 = shift(jnp.concatenate([b3[0:256], b3[576:896]], axis=0), -1)
    sp, se = step(3, n3, n2, sp, se)
    n4 = (a4, flip_c(a4), b4, flip_c(b4))
    a5, b5 = shift(a4[320:448], 1), shift(b4[384:576], -1)
    sp, se, send = step(4, n4, n3, sp, se)
    got = flip_y(send)
    n5 = (a5, flip_c(a5), b5, flip_c(b5))
    local_context = pl.pallas_call(
        last_body,
        out_shape=arr((320, 896)),
        in_specs=[SMEM] + [VMEM] * 10,
        out_specs=VMEM,
        scratch_shapes=[pltpu.VMEM((1792, 384), F32)],
        compiler_params=params(),
        cost_estimate=cost(5e8, 1e6, 4e6),
        name="last",
    )(idx, qs, a4, n4[1], *n5, sp, se, got)
    context = lax.all_to_all(local_context, "tp", split_axis=0, concat_axis=1, tiled=True)

    new_pool = pl.pallas_call(
        pages_body,
        out_shape=arr((6, 128, 256)),
        in_specs=[SMEM, SMEM] + [ANY] * 25,
        out_specs=ANY,
        scratch_shapes=[pltpu.SMEM((6,), jnp.int32), pltpu.SemaphoreType.DMA((6,))],
        compiler_params=params(),
        name="pages",
    )(idx, page_slot_table, pages, x, xc, yp, yc, *n1, *n2, *n3, *n4, *n5)
    return context, new_pool.reshape(6, 128, 1, 256)


def solution(mesh):
    in_specs = (
        P("ctx", "tp"),
        P("ctx", "tp", None),
        P("ctx", "tp"),
        P("ctx", "tp", None),
        P("ctx", None, "tp", None),
        P(),
    )
    out_specs = (P(("ctx", "tp"), None), P("ctx", None, "tp", None))
    return jax.shard_map(body, mesh=mesh, in_specs=in_specs, out_specs=out_specs, check_vma=False)
```

```python
import jax
import jax.numpy as jnp
from jax import lax
from jax.experimental import pallas as pl
from jax.experimental.pallas import tpu as pltpu
from jax.sharding import PartitionSpec as P

HEADS = 7
HD = 128
NEG = -1e30
C1 = 1.4426950408889634 * HD ** -0.5
F32 = jnp.float32
BF = jnp.bfloat16

VMEM = pl.BlockSpec(memory_space=pltpu.VMEM)
SMEM = pl.BlockSpec(memory_space=pltpu.SMEM)
ANY = pl.BlockSpec(memory_space=pl.ANY)
HBM = pl.BlockSpec(memory_space=pltpu.HBM)


def params():
    return pltpu.CompilerParams(vmem_limit_bytes=20 << 20)


def cost(flops, elems, nbytes):
    return pl.CostEstimate(flops=int(flops), transcendentals=int(elems), bytes_accessed=int(nbytes))


def update(q_ref, q0, state, rows, chunk, blocks, fix=None, source=None):
    source = state if source is None else source
    kv = blocks[0] if len(blocks) == 1 else jnp.concatenate(blocks, axis=0)
    keys = kv[:, :HD]
    values = jnp.concatenate([jnp.ones((kv.shape[0], HD), BF), kv[:, HD:]], axis=1)
    for r in range(0, rows, chunk):
        at = pl.ds(q0 + r, chunk)
        s = lax.dot_general(
            q_ref[at, :], keys, (((1,), (1,)), ((), ())), preferred_element_type=F32
        )
        if fix is not None:
            s = fix(s, r)
        m_old = source[at, :HD]
        m_new = jnp.maximum(m_old, jnp.max(s, axis=1, keepdims=True))
        p = jnp.exp2((s - jnp.concatenate([m_new] * (s.shape[1] // HD), axis=1)) * C1).astype(BF)
        alpha = jnp.exp2((m_old - m_new) * C1)
        pv = lax.dot_general(p, values, (((1,), (0,)), ((), ())), preferred_element_type=F32)
        state[at, :HD] = m_new
        state[at, HD:] = source[at, HD:] * jnp.concatenate([alpha, alpha], axis=1) + pv


def position(idx_ref):
    i = idx_ref[0]
    return i // 4, (i // 2) % 2, i % 2


def prep_body(idx_ref, table_ref, pool_ref, kvp_ref, kve_ref, qe_ref, x_ref, p_ref, sems):
    base = idx_ref[0] * 6

    def scan(j, found):
        n, a, b = found
        local = table_ref[j] - base
        inside = (local >= 0) & (local < 6)
        a = jnp.where(inside & (n == 0), local, a)
        b = jnp.where(inside & (n == 1), local, b)
        return n + inside.astype(jnp.int32), a, b

    zero = jnp.int32(0)
    early = [
        pltpu.make_async_copy(kvp_ref, x_ref.at[256:512], sems.at[0]),
        pltpu.make_async_copy(kve_ref, x_ref.at[512:576], sems.at[1]),
        pltpu.make_async_copy(kvp_ref, p_ref.at[0:256], sems.at[2]),
        pltpu.make_async_copy(kve_ref, p_ref.at[256:320], sems.at[3]),
    ]
    for h in range(HEADS):
        to = p_ref.at[320 + h // 2 * 64:384 + h // 2 * 64, h % 2 * HD:h % 2 * HD + HD]
        early.append(pltpu.make_async_copy(qe_ref.at[:, h * HD:(h + 1) * HD], to, sems.at[6 + h]))
    for copy in early:
        copy.start()
    _, a, b = lax.fori_loop(0, 64, scan, (zero, zero, zero))
    late = [
        pltpu.make_async_copy(pool_ref.at[a], x_ref.at[0:128], sems.at[4]),
        pltpu.make_async_copy(pool_ref.at[b], x_ref.at[128:256], sems.at[5]),
    ]
    for copy in late:
        copy.start()
    for copy in early + late:
        copy.wait()


def page_copies(idx_ref, table_ref, pool_ref, sems, items):
    base = idx_ref[0] * 6
    waits = []

    def add(entry, ref, row, count, to):
        local = table_ref[entry] - base
        go = (local >= 0) & (local < 6)
        sem = sems.at[len(waits)]

        def copy():
            return pltpu.make_async_copy(
                ref.at[row:row + count], pool_ref.at[local, pl.ds(to, count)], sem
            )

        @pl.when(go)
        def _():
            copy().start()

        waits.append((go, copy))

    for shard, ref, front, back, ext in items:
        if front is not None:
            add(80 + shard, ref, front, 128, 0)
        if back is not None:
            add(143 - shard, ref, back, 128, 0)
        if ext is not None:
            add(64 + shard // 2, ref, ext, 64, pl.multiple_of(shard % 2 * 64, 64))

    def wait():
        for go, copy in waits:
            @pl.when(go)
            def _(copy=copy):
                copy().wait()

    return wait


def shard_at(idx_ref, plane):
    return 4 * plane + idx_ref[0] % 4


def ext_plane(z, plane, qx_ref, se_ref, kv):
    bias = jnp.full((1, 128), jnp.where(plane < z, 0.0, NEG), F32)

    def fix(s, _):
        return jnp.concatenate([s[:, :512], s[:, 512:] + bias], axis=1)

    update(qx_ref, 0, se_ref, 896, 448, [kv[...]], fix)


def ext_planes(z, minus, plus, qx_ref, se_ref, kv_ref, parts):
    for i, (r, rc) in enumerate(parts):
        kv_ref[i, 0:256, :] = r[0:256, :]
        kv_ref[i, 256:512, :] = rc[0:256, :]
        kv_ref[i, 512:576, :] = r[512:576, :]
        kv_ref[i, 576:640, :] = rc[512:576, :]

    def one(i, carry):
        ext_plane(z, jnp.where(i == 0, minus, plus), qx_ref, se_ref, kv_ref.at[i])
        return carry

    lax.fori_loop(0, 2, one, 0)


def first_body(
    idx_ref, table_ref, qp_ref, qe_ref, x_ref, xc_ref, y_ref, yc_ref, a_ref, ac_ref, b_ref, bc_ref, pool_ref,
    qs_ref, qx_ref, sp_ref, se_ref, out_ref, token_ref, kv_ref, sems,
):
    z, y, c = position(idx_ref)
    j = 2 * y + c
    whole = pltpu.make_async_copy(pool_ref, out_ref, sems.at[24])
    whole.start()
    for h in range(HEADS):
        cols = slice(h * HD, (h + 1) * HD)
        qs_ref[h * 128:(h + 1) * 128, :] = qp_ref[0:128, cols]
        qs_ref[896 + h * 128:896 + (h + 1) * 128, :] = qp_ref[128:256, cols]
        qx_ref[h * 64:(h + 1) * 64, :] = qe_ref[:, cols]
        qx_ref[448 + h * 64:448 + (h + 1) * 64, :] = y_ref[320 + h // 2 * 64:384 + h // 2 * 64, h % 2 * HD:h % 2 * HD + HD]
    for state in (sp_ref, se_ref):
        state[:, :HD] = jnp.full((state.shape[0], HD), NEG, F32)
        state[:, HD:] = jnp.zeros((state.shape[0], 2 * HD), F32)
    whole.wait()
    minus = (z + 7) % 8
    plus = (z + 1) % 8
    own = idx_ref[0]
    am, bm = shard_at(idx_ref, minus), shard_at(idx_ref, plus)
    wait = page_copies(
        idx_ref, table_ref, out_ref, sems,
        [
            (own, x_ref, 256, 384, 512), (own ^ 1, xc_ref, 256, 384, 512),
            (own ^ 2, y_ref, 0, 128, 256), (own ^ 3, yc_ref, 0, 128, 256),
            (am, a_ref, 256, 384, 512), (am ^ 1, ac_ref, 256, 384, 512),
            (bm, b_ref, 256, 384, 512), (bm ^ 1, bc_ref, 256, 384, 512),
        ],
    )

    def shown(seen, width):
        return jnp.full((1, width), jnp.where(seen, 0.0, NEG), F32)

    rows = lax.broadcasted_iota(jnp.int32, (128, 128), 0)
    lanes = lax.broadcasted_iota(jnp.int32, (128, 128), 1)
    causal = jnp.where(rows >= lanes, 0.0, NEG).astype(F32)
    others = (j ^ 1, j ^ 2, j ^ 3)
    front = jnp.concatenate([shown(o < j, 128) for o in others], axis=1)
    back = jnp.concatenate([shown(o > j, 128) for o in others], axis=1)

    def fix_front(s, r):
        return jnp.concatenate([s[:, :128] + causal, s[:, 128:] + front], axis=1)

    def fix_back(s, r):
        return jnp.concatenate([s[:, :512], s[:, 512:640] + causal, s[:, 640:] + back], axis=1)

    firsts = [x_ref[256:384, :], xc_ref[256:384, :], y_ref[0:128, :], yc_ref[0:128, :]]
    seconds = [x_ref[384:512, :], xc_ref[384:512, :], y_ref[128:256, :], yc_ref[128:256, :]]
    update(qs_ref, 0, sp_ref, 896, 128, firsts, fix_front)
    update(qs_ref, 896, sp_ref, 896, 128, firsts + seconds, fix_back)

    tokens = lax.broadcasted_iota(jnp.int32, (448, 128), 0) % 64
    slots = lax.broadcasted_iota(jnp.int32, (448, 128), 1)
    mine = jnp.where(
        slots < 64,
        jnp.where(tokens >= slots, 0.0, NEG).astype(F32),
        jnp.full((448, 128), jnp.where(c == 1, 0.0, NEG), F32),
    )
    mate = shown(y == 0, 128)

    def fix_ext(s, r):
        tail = s[:, 512:] + (mine if r == 0 else mate)
        return jnp.concatenate([s[:, :512], tail], axis=1)

    update(
        qx_ref, 0, se_ref, 896, 448,
        [x_ref[0:256, :], xc_ref[0:256, :], x_ref[512:576, :], xc_ref[512:576, :]], fix_ext,
    )
    ext_planes(z, minus, plus, qx_ref, se_ref, kv_ref, [(a_ref, ac_ref), (b_ref, bc_ref)])
    token_ref[...] = jnp.zeros((8, 128), F32)
    wait()


def selected(z, planes, qs_ref, sp_ref, kv_ref, parts):
    for i, (plane, blocks) in enumerate(zip(planes, parts)):
        for side in range(2):
            @pl.when((plane > z) == (side == 1))
            def _(i=i, side=side, blocks=blocks):
                for n, block in enumerate(blocks):
                    ref, row = block[side]
                    kv_ref[i, n * 128:(n + 1) * 128, :] = ref[row:row + 128, :]

    def one(i, carry):
        plane = planes[0] if len(planes) == 1 else jnp.where(i == 0, planes[0], planes[1])
        q0 = pl.multiple_of(jnp.where(plane > z, 896, 0), 128)
        update(qs_ref, q0, sp_ref, 896, 128, [kv_ref[i, 0:512, :]])
        return carry

    if len(planes) == 1:
        one(0, 0)
    else:
        lax.fori_loop(0, 2, one, 0)


def around(idx_ref, k):
    z, _, _ = position(idx_ref)
    return z, (z + 8 - k) % 8, (z + k) % 8


def prompt_planes(idx_ref, k, now, before, y_rows, qs_ref, sp_in, sp_ref, kv_ref):
    z, minus, plus = around(idx_ref, k - 1)
    sp_ref[0:896, :] = sp_in[0:896, :]
    parts = []
    for i in range(2):
        shards = [(before[2 * i], 256), (before[2 * i + 1], 256), (now[2 * i], y_rows[i]), (now[2 * i + 1], y_rows[i])]
        parts.append([((ref, row), (ref, row + 128)) for ref, row in shards])
    fronts = [ref[row:row + 128, :] for plane in parts for (ref, row), _ in plane]
    update(qs_ref, 896, sp_ref, 896, 128, fronts, source=sp_in)
    selected(z, (minus, plus), qs_ref, sp_ref, kv_ref, parts)


def step_items(idx_ref, k, now, y_rows):
    _, minus, plus = around(idx_ref, k)
    _, minus1, plus1 = around(idx_ref, k - 1)
    am, bm = shard_at(idx_ref, minus), shard_at(idx_ref, plus)
    am1, bm1 = shard_at(idx_ref, minus1) ^ 2, shard_at(idx_ref, plus1) ^ 2
    fa, fac, fb, fbc = now
    if k < 4:
        items = [
            (am, fa, 256, 384, 512), (am ^ 1, fac, 256, 384, 512),
            (bm, fb, 256, 384, 512), (bm ^ 1, fbc, 256, 384, 512),
        ]
    else:
        items = [(am, fa, 0, 128, 256), (am ^ 1, fac, 0, 128, 256)]
    ya, yb = y_rows
    return items + [
        (am1, fa, ya, ya + 128, ya + 256), (am1 ^ 1, fac, ya, ya + 128, ya + 256),
        (bm1, fb, yb, yb + 128, yb + 256), (bm1 ^ 1, fbc, yb, yb + 128, yb + 256),
    ]


def step_body(k, *refs):
    idx_ref, table_ref, qs_ref, qx_ref = refs[:4]
    now, before = refs[4:8], refs[8:12]
    sp_in, se_in, _, sp_ref, se_ref, out_ref, token_ref, kv_ref, sems = refs[12:]
    y_rows = (576, 576)
    wait = page_copies(idx_ref, table_ref, out_ref, sems, step_items(idx_ref, k, now, y_rows))
    z, minus, plus = around(idx_ref, k)
    se_ref[...] = se_in[...]
    ext_planes(z, minus, plus, qx_ref, se_ref, kv_ref, [now[0:2], now[2:4]])
    prompt_planes(idx_ref, k, now, before, y_rows, qs_ref, sp_in, sp_ref, kv_ref)
    token_ref[...] = jnp.zeros((8, 128), F32)
    wait()


def ext_last_body(idx_ref, qx_ref, fa, fac, fb, fbc, se_in, se_ref, send_ref, kv_ref):
    z, _, plus = around(idx_ref, 4)
    se_ref[...] = se_in[...]
    kv_ref[0, 0:256, :] = fb[0:256, :]
    kv_ref[0, 256:512, :] = fbc[0:256, :]
    kv_ref[0, 512:576, :] = fa[256:320, :]
    kv_ref[0, 576:640, :] = fac[256:320, :]
    ext_plane(z, plus, qx_ref, se_ref, kv_ref.at[0])
    part = se_ref[448:896, :]
    total = part[:, HD:2 * HD]
    level = part[:, :HD] * C1 + jnp.log2(total)
    hi = level.astype(BF)
    rest = level - hi.astype(F32)
    mid = rest.astype(BF)
    low = (rest - mid.astype(F32)).astype(BF)
    lane = lax.broadcasted_iota(jnp.int32, (448, HD), 1)
    stats = jnp.where(
        lane == 0, hi.astype(F32), jnp.where(lane == 1, mid.astype(F32), low.astype(F32))
    )
    send_ref[:, :HD] = (part[:, 2 * HD:] / total).astype(BF)
    send_ref[:, HD:] = stats.astype(BF)


def prompt4_body(idx_ref, table_ref, qs_ref, *refs):
    now, before = refs[:4], refs[4:8]
    sp_in, _, sp_ref, out_ref, kv_ref, sems = refs[8:]
    y_rows = (320, 256)
    wait = page_copies(idx_ref, table_ref, out_ref, sems, step_items(idx_ref, 4, now, y_rows))
    prompt_planes(idx_ref, 4, now, before, y_rows, qs_ref, sp_in, sp_ref, kv_ref)
    wait()


def last_body(
    idx_ref, table_ref, qs_ref, g_ref, gc_ref, ra_ref, rac_ref, rb_ref, rbc_ref, sp_in, se_ref, got_ref, _,
    out_ref, pool_ref, sp_ref, kv_ref, sems,
):
    z, _, _ = position(idx_ref)
    plane = (z + 4) % 8
    shard = shard_at(idx_ref, plane) ^ 2
    wait = page_copies(
        idx_ref, table_ref, pool_ref, sems,
        [
            (shard, ra_ref, 0, None, None), (shard ^ 1, rac_ref, 0, None, None),
            (shard, rb_ref, None, 0, 128), (shard ^ 1, rbc_ref, None, 0, 128),
        ],
    )
    firsts = [g_ref[0:128, :], gc_ref[0:128, :], ra_ref[...], rac_ref[...]]
    sp_ref[0:896, :] = sp_in[0:896, :]
    update(qs_ref, 896, sp_ref, 896, 128, firsts, source=sp_in)
    blocks = [
        ((g_ref, 0), (g_ref, 128)), ((gc_ref, 0), (gc_ref, 128)), ((ra_ref, 0), (rb_ref, 0)), ((rac_ref, 0), (rbc_ref, 0))
    ]
    selected(z, (plane,), qs_ref, sp_ref, kv_ref, [blocks])

    for b in range(2):
        for h in range(HEADS):
            at = slice(b * 896 + h * 128, b * 896 + (h + 1) * 128)
            out_ref[b * 128:(b + 1) * 128, h * HD:(h + 1) * HD] = (
                sp_ref[at, 2 * HD:] / sp_ref[at, HD:2 * HD]
            ).astype(BF)
    for h in range(HEADS):
        at = slice(h * 64, (h + 1) * 64)
        total = se_ref[at, HD:2 * HD]
        level = se_ref[at, :HD] * C1 + jnp.log2(total)
        mine = se_ref[at, 2 * HD:] / total
        got = got_ref[at, :].astype(F32)
        level_y = got[:, HD:HD + 1] + got[:, HD + 1:HD + 2] + got[:, HD + 2:HD + 3]
        top = jnp.maximum(level, level_y)
        wa = jnp.exp2(level - top)
        wb = jnp.exp2(level_y - top)
        out_ref[256:320, h * HD:(h + 1) * HD] = (
            (wa * mine + wb * got[:, :HD]) / (wa + wb)
        ).astype(BF)
    wait()


def body(q_prompt, kv_prompt, q_ext, kv_ext, pool, page_slot_table):
    idx = lax.axis_index("ctx").astype(jnp.int32).reshape(1)
    kvp = kv_prompt.reshape(256, 256)
    kve = kv_ext.reshape(64, 256)
    pages = pool.reshape(6, 128, 256)

    def shift(x, d):
        return lax.ppermute(x, "ctx", [(i, (i + 4 * d) % 32) for i in range(32)])

    def flip_y(x):
        return lax.ppermute(x, "ctx", [(i, i ^ 2) for i in range(32)])

    def flip_c(x):
        return lax.ppermute(x, "ctx", [(i, i ^ 1) for i in range(32)])

    def after(x, token):
        return lax.optimization_barrier((x, token))[0]

    def arr(shape, dtype=BF):
        return jax.ShapeDtypeStruct(shape, dtype)

    def hbm(x):
        return pltpu.with_memory_space_constraint(x, pltpu.HBM)

    x, p = pl.pallas_call(
        prep_body,
        out_shape=(arr((576, 256)), arr((576, 256))),
        in_specs=[SMEM, SMEM, HBM, HBM, HBM, HBM],
        out_specs=(ANY, ANY),
        scratch_shapes=[pltpu.SemaphoreType.DMA((13,))],
        compiler_params=params(),
        name="prep",
    )(idx, page_slot_table, hbm(pages), hbm(kvp), hbm(kve), hbm(q_ext))

    yp = flip_y(p)
    a1, b1 = shift(x, 1), shift(x, -1)
    xc, yc = flip_c(x), flip_c(yp)
    n1 = (a1, flip_c(a1), b1, flip_c(b1))
    a2 = shift(jnp.concatenate([a1, yp[:320]], axis=0), 1)
    b2 = shift(jnp.concatenate([b1, yp[:320]], axis=0), -1)

    sp_t, se_t, pool_t = arr((1792, 384), F32), arr((896, 384), F32), arr((6, 128, 256))
    token_t = arr((8, 128), F32)
    sems = pltpu.SemaphoreType.DMA((25,))
    kv_t = pltpu.VMEM((2, 640, 256), BF)
    qs, qx, sp, se, new_pool, token = pl.pallas_call(
        first_body,
        out_shape=(arr((1792, 128)), arr((896, 128)), sp_t, se_t, pool_t, token_t),
        in_specs=[SMEM, SMEM] + [VMEM] * 11,
        out_specs=(VMEM,) * 4 + (HBM, VMEM),
        scratch_shapes=[kv_t, sems],
        compiler_params=params(),
        cost_estimate=cost(2e9, 3e6, 4e6),
        name="step1",
    )(idx, page_slot_table, q_prompt, q_ext, x, xc, yp, yc, *n1, pages)

    def step(k, now, before, sp, se, new_pool):
        return pl.pallas_call(
            lambda *refs: step_body(k, *refs),
            out_shape=(sp_t, se_t, pool_t, token_t),
            in_specs=[SMEM, SMEM] + [VMEM] * 12 + [HBM],
            out_specs=(VMEM, VMEM, HBM, VMEM),
            input_output_aliases={12: 0, 13: 1, 14: 2},
            scratch_shapes=[kv_t, sems],
            compiler_params=params(),
            cost_estimate=cost(2e9, 3e6, 8e6),
            name=f"step{k}",
        )(idx, page_slot_table, qs, qx, *now, *before, sp, se, new_pool)

    a2, b2 = after(a2, token), after(b2, token)
    a3, b3 = shift(a2, 1), shift(b2, -1)
    n2 = (a2, flip_c(a2), b2, flip_c(b2))
    sp, se, new_pool, token = step(2, n2, n1, sp, se, new_pool)
    a3, b3 = after(a3, token), after(b3, token)
    a4 = shift(a3[256:896], 1)
    b4 = shift(jnp.concatenate([b3[0:256], b3[576:896]], axis=0), -1)
    n3 = (a3, flip_c(a3), b3, flip_c(b3))
    sp, se, new_pool, token = step(3, n3, n2, sp, se, new_pool)
    a4, b4 = after(a4, token), after(b4, token)
    a5 = shift(a4[320:448], 1)
    b5 = shift(b4[384:576], -1)
    n4 = (a4, flip_c(a4), b4, flip_c(b4))
    se, send = pl.pallas_call(
        ext_last_body,
        out_shape=(se_t, arr((448, 256))),
        in_specs=[SMEM] + [VMEM] * 6,
        out_specs=(VMEM, VMEM),
        input_output_aliases={6: 0},
        scratch_shapes=[kv_t],
        compiler_params=params(),
        cost_estimate=cost(3e8, 6e5, 3e6),
        name="ext4",
    )(idx, qx, *n4, se)
    got = flip_y(send)
    sp, new_pool = pl.pallas_call(
        prompt4_body,
        out_shape=(sp_t, pool_t),
        in_specs=[SMEM, SMEM] + [VMEM] * 10 + [HBM],
        out_specs=(VMEM, HBM),
        input_output_aliases={11: 0, 12: 1},
        scratch_shapes=[kv_t, sems],
        compiler_params=params(),
        cost_estimate=cost(2e9, 2e6, 6e6),
        name="prompt4",
    )(idx, page_slot_table, qs, *n4, *n3, sp, new_pool)
    local_context, new_pool = pl.pallas_call(
        last_body,
        out_shape=(arr((320, 896)), pool_t),
        in_specs=[SMEM, SMEM] + [VMEM] * 10 + [HBM],
        out_specs=(VMEM, HBM),
        input_output_aliases={12: 1},
        scratch_shapes=[pltpu.VMEM((1792, 384), F32), kv_t, sems],
        compiler_params=params(),
        cost_estimate=cost(5e8, 1e6, 4e6),
        name="last",
    )(idx, page_slot_table, qs, a4, n4[1], a5, flip_c(a5), b5, flip_c(b5), sp, se, got, new_pool)
    context = lax.all_to_all(local_context, "tp", split_axis=0, concat_axis=1, tiled=True)
    return context, new_pool.reshape(6, 128, 1, 256)


def solution(mesh):
    in_specs = (
        P("ctx", "tp"),
        P("ctx", "tp", None),
        P("ctx", "tp"),
        P("ctx", "tp", None),
        P("ctx", None, "tp", None),
        P(),
    )
    out_specs = (P(("ctx", "tp"), None), P("ctx", None, "tp", None))
    return jax.shard_map(body, mesh=mesh, in_specs=in_specs, out_specs=out_specs, check_vma=False)
```

```python
import jax
import jax.numpy as jnp
from jax import lax
from jax.experimental import pallas as pl
from jax.experimental.pallas import tpu as pltpu
from jax.sharding import PartitionSpec as P

HEADS = 7
HD = 128
NEG = -1e30
C1 = 1.4426950408889634 * HD ** -0.5
F32 = jnp.float32
BF = jnp.bfloat16

VMEM = pl.BlockSpec(memory_space=pltpu.VMEM)
SMEM = pl.BlockSpec(memory_space=pltpu.SMEM)
ANY = pl.BlockSpec(memory_space=pl.ANY)
HBM = pl.BlockSpec(memory_space=pltpu.HBM)


def params():
    return pltpu.CompilerParams(vmem_limit_bytes=20 << 20)


def cost(flops, elems, nbytes):
    return pl.CostEstimate(flops=int(flops), transcendentals=int(elems), bytes_accessed=int(nbytes))


def update(q_ref, q0, state, rows, chunk, blocks, fix=None, source=None):
    source = state if source is None else source
    kv = blocks[0] if len(blocks) == 1 else jnp.concatenate(blocks, axis=0)
    keys = kv[:, :HD]
    values = jnp.concatenate([jnp.ones((kv.shape[0], HD), BF), kv[:, HD:]], axis=1)
    for r in range(0, rows, chunk):
        at = pl.ds(q0 + r, chunk)
        s = lax.dot_general(
            q_ref[at, :], keys, (((1,), (1,)), ((), ())), preferred_element_type=F32
        )
        if fix is not None:
            s = fix(s, r)
        m_old = source[at, :HD]
        m_new = jnp.maximum(m_old, jnp.max(s, axis=1, keepdims=True))
        p = jnp.exp2((s - jnp.concatenate([m_new] * (s.shape[1] // HD), axis=1)) * C1).astype(BF)
        alpha = jnp.exp2((m_old - m_new) * C1)
        pv = lax.dot_general(p, values, (((1,), (0,)), ((), ())), preferred_element_type=F32)
        state[at, :HD] = m_new
        state[at, HD:] = source[at, HD:] * jnp.concatenate([alpha, alpha], axis=1) + pv


def position(idx_ref):
    i = idx_ref[0]
    return i // 4, (i // 2) % 2, i % 2


def prep_body(idx_ref, table_ref, pool_ref, kvp_ref, kve_ref, qe_ref, x_ref, p_ref, sems):
    base = idx_ref[0] * 6

    def scan(j, found):
        n, a, b = found
        local = table_ref[j] - base
        inside = (local >= 0) & (local < 6)
        a = jnp.where(inside & (n == 0), local, a)
        b = jnp.where(inside & (n == 1), local, b)
        return n + inside.astype(jnp.int32), a, b

    zero = jnp.int32(0)
    early = [
        pltpu.make_async_copy(kvp_ref, x_ref.at[256:512], sems.at[0]),
        pltpu.make_async_copy(kve_ref, x_ref.at[512:576], sems.at[1]),
        pltpu.make_async_copy(kvp_ref, p_ref.at[0:256], sems.at[2]),
        pltpu.make_async_copy(kve_ref, p_ref.at[256:320], sems.at[3]),
    ]
    for h in range(HEADS):
        to = p_ref.at[320 + h // 2 * 64:384 + h // 2 * 64, h % 2 * HD:h % 2 * HD + HD]
        early.append(pltpu.make_async_copy(qe_ref.at[:, h * HD:(h + 1) * HD], to, sems.at[6 + h]))
    for copy in early:
        copy.start()
    found = (zero, zero, zero)
    for j in range(64):
        found = scan(j, found)
    _, a, b = found
    late = [
        pltpu.make_async_copy(pool_ref.at[a], x_ref.at[0:128], sems.at[4]),
        pltpu.make_async_copy(pool_ref.at[b], x_ref.at[128:256], sems.at[5]),
    ]
    for copy in late:
        copy.start()
    for copy in early + late:
        copy.wait()


def page_copies(idx_ref, table_ref, pool_ref, sems, items):
    base = idx_ref[0] * 6
    waits = []

    def add(entry, ref, row, count, to):
        local = table_ref[entry] - base
        go = (local >= 0) & (local < 6)
        sem = sems.at[len(waits)]

        def copy():
            return pltpu.make_async_copy(
                ref.at[row:row + count], pool_ref.at[local, pl.ds(to, count)], sem
            )

        @pl.when(go)
        def _():
            copy().start()

        waits.append((go, copy))

    for shard, ref, front, back, ext in items:
        if front is not None:
            add(80 + shard, ref, front, 128, 0)
        if back is not None:
            add(143 - shard, ref, back, 128, 0)
        if ext is not None:
            add(64 + shard // 2, ref, ext, 64, pl.multiple_of(shard % 2 * 64, 64))

    def wait():
        for go, copy in waits:
            @pl.when(go)
            def _(copy=copy):
                copy().wait()

    return wait


def shard_at(idx_ref, plane):
    return 4 * plane + idx_ref[0] % 4


def ext_plane(z, plane, qx_ref, se_ref, kv):
    bias = jnp.full((1, 128), jnp.where(plane < z, 0.0, NEG), F32)

    def fix(s, _):
        return jnp.concatenate([s[:, :512], s[:, 512:] + bias], axis=1)

    update(qx_ref, 0, se_ref, 896, 448, [kv[...]], fix)


def ext_planes(z, minus, plus, qx_ref, se_ref, kv_ref, parts):
    for i, (r, rc) in enumerate(parts):
        kv_ref[i, 0:256, :] = r[0:256, :]
        kv_ref[i, 256:512, :] = rc[0:256, :]
        kv_ref[i, 512:576, :] = r[512:576, :]
        kv_ref[i, 576:640, :] = rc[512:576, :]

    def one(i, carry):
        ext_plane(z, jnp.where(i == 0, minus, plus), qx_ref, se_ref, kv_ref.at[i])
        return carry

    lax.fori_loop(0, 2, one, 0)


def first_body(
    idx_ref, table_ref, qp_ref, qe_ref, x_ref, xc_ref, y_ref, yc_ref, a_ref, ac_ref, b_ref, bc_ref, pool_ref,
    qs_ref, qx_ref, sp_ref, se_ref, out_ref, token_ref, kv_ref, sems,
):
    z, y, c = position(idx_ref)
    j = 2 * y + c
    whole = pltpu.make_async_copy(pool_ref, out_ref, sems.at[24])
    whole.start()
    for h in range(HEADS):
        cols = slice(h * HD, (h + 1) * HD)
        qs_ref[h * 128:(h + 1) * 128, :] = qp_ref[0:128, cols]
        qs_ref[896 + h * 128:896 + (h + 1) * 128, :] = qp_ref[128:256, cols]
        qx_ref[h * 64:(h + 1) * 64, :] = qe_ref[:, cols]
        qx_ref[448 + h * 64:448 + (h + 1) * 64, :] = y_ref[320 + h // 2 * 64:384 + h // 2 * 64, h % 2 * HD:h % 2 * HD + HD]
    for state in (sp_ref, se_ref):
        state[:, :HD] = jnp.full((state.shape[0], HD), NEG, F32)
        state[:, HD:] = jnp.zeros((state.shape[0], 2 * HD), F32)
    whole.wait()
    minus = (z + 7) % 8
    plus = (z + 1) % 8
    own = idx_ref[0]
    am, bm = shard_at(idx_ref, minus), shard_at(idx_ref, plus)
    wait = page_copies(
        idx_ref, table_ref, out_ref, sems,
        [
            (own, x_ref, 256, 384, 512), (own ^ 1, xc_ref, 256, 384, 512),
            (own ^ 2, y_ref, 0, 128, 256), (own ^ 3, yc_ref, 0, 128, 256),
            (am, a_ref, 256, 384, 512), (am ^ 1, ac_ref, 256, 384, 512),
            (bm, b_ref, 256, 384, 512), (bm ^ 1, bc_ref, 256, 384, 512),
        ],
    )

    def shown(seen, width):
        return jnp.full((1, width), jnp.where(seen, 0.0, NEG), F32)

    rows = lax.broadcasted_iota(jnp.int32, (128, 128), 0)
    lanes = lax.broadcasted_iota(jnp.int32, (128, 128), 1)
    causal = jnp.where(rows >= lanes, 0.0, NEG).astype(F32)
    others = (j ^ 1, j ^ 2, j ^ 3)
    front = jnp.concatenate([shown(o < j, 128) for o in others], axis=1)
    back = jnp.concatenate([shown(o > j, 128) for o in others], axis=1)

    def fix_front(s, r):
        return jnp.concatenate([s[:, :128] + causal, s[:, 128:] + front], axis=1)

    def fix_back(s, r):
        return jnp.concatenate([s[:, :512], s[:, 512:640] + causal, s[:, 640:] + back], axis=1)

    firsts = [x_ref[256:384, :], xc_ref[256:384, :], y_ref[0:128, :], yc_ref[0:128, :]]
    seconds = [x_ref[384:512, :], xc_ref[384:512, :], y_ref[128:256, :], yc_ref[128:256, :]]
    update(qs_ref, 0, sp_ref, 896, 128, firsts, fix_front)
    update(qs_ref, 896, sp_ref, 896, 128, firsts + seconds, fix_back)

    tokens = lax.broadcasted_iota(jnp.int32, (448, 128), 0) % 64
    slots = lax.broadcasted_iota(jnp.int32, (448, 128), 1)
    mine = jnp.where(
        slots < 64,
        jnp.where(tokens >= slots, 0.0, NEG).astype(F32),
        jnp.full((448, 128), jnp.where(c == 1, 0.0, NEG), F32),
    )
    mate = shown(y == 0, 128)

    def fix_ext(s, r):
        tail = s[:, 512:] + (mine if r == 0 else mate)
        return jnp.concatenate([s[:, :512], tail], axis=1)

    update(
        qx_ref, 0, se_ref, 896, 448,
        [x_ref[0:256, :], xc_ref[0:256, :], x_ref[512:576, :], xc_ref[512:576, :]], fix_ext,
    )
    ext_planes(z, minus, plus, qx_ref, se_ref, kv_ref, [(a_ref, ac_ref), (b_ref, bc_ref)])
    token_ref[...] = jnp.zeros((8, 128), F32)
    wait()


def selected(z, planes, qs_ref, sp_ref, kv_ref, parts):
    for i, (plane, blocks) in enumerate(zip(planes, parts)):
        for side in range(2):
            @pl.when((plane > z) == (side == 1))
            def _(i=i, side=side, blocks=blocks):
                for n, block in enumerate(blocks):
                    ref, row = block[side]
                    kv_ref[i, n * 128:(n + 1) * 128, :] = ref[row:row + 128, :]

    def one(i, carry):
        plane = planes[0] if len(planes) == 1 else jnp.where(i == 0, planes[0], planes[1])
        q0 = pl.multiple_of(jnp.where(plane > z, 896, 0), 128)
        update(qs_ref, q0, sp_ref, 896, 128, [kv_ref[i, 0:512, :]])
        return carry

    if len(planes) == 1:
        one(0, 0)
    else:
        lax.fori_loop(0, 2, one, 0)


def around(idx_ref, k):
    z, _, _ = position(idx_ref)
    return z, (z + 8 - k) % 8, (z + k) % 8


def prompt_planes(idx_ref, k, now, before, y_rows, qs_ref, sp_in, sp_ref, kv_ref):
    z, minus, plus = around(idx_ref, k - 1)
    sp_ref[0:896, :] = sp_in[0:896, :]
    parts = []
    for i in range(2):
        shards = [(before[2 * i], 256), (before[2 * i + 1], 256), (now[2 * i], y_rows[i]), (now[2 * i + 1], y_rows[i])]
        parts.append([((ref, row), (ref, row + 128)) for ref, row in shards])
    fronts = [ref[row:row + 128, :] for plane in parts for (ref, row), _ in plane]
    update(qs_ref, 896, sp_ref, 896, 128, fronts, source=sp_in)
    selected(z, (minus, plus), qs_ref, sp_ref, kv_ref, parts)


def step_items(idx_ref, k, now, y_rows):
    _, minus, plus = around(idx_ref, k)
    _, minus1, plus1 = around(idx_ref, k - 1)
    am, bm = shard_at(idx_ref, minus), shard_at(idx_ref, plus)
    am1, bm1 = shard_at(idx_ref, minus1) ^ 2, shard_at(idx_ref, plus1) ^ 2
    fa, fac, fb, fbc = now
    if k < 4:
        items = [
            (am, fa, 256, 384, 512), (am ^ 1, fac, 256, 384, 512),
            (bm, fb, 256, 384, 512), (bm ^ 1, fbc, 256, 384, 512),
        ]
    else:
        items = [(am, fa, 0, 128, 256), (am ^ 1, fac, 0, 128, 256)]
    ya, yb = y_rows
    return items + [
        (am1, fa, ya, ya + 128, ya + 256), (am1 ^ 1, fac, ya, ya + 128, ya + 256),
        (bm1, fb, yb, yb + 128, yb + 256), (bm1 ^ 1, fbc, yb, yb + 128, yb + 256),
    ]


def step_body(k, *refs):
    idx_ref, table_ref, qs_ref, qx_ref = refs[:4]
    now, before = refs[4:8], refs[8:12]
    sp_in, se_in, _, sp_ref, se_ref, out_ref, token_ref, kv_ref, sems = refs[12:]
    y_rows = (576, 576)
    wait = page_copies(idx_ref, table_ref, out_ref, sems, step_items(idx_ref, k, now, y_rows))
    z, minus, plus = around(idx_ref, k)
    se_ref[...] = se_in[...]
    ext_planes(z, minus, plus, qx_ref, se_ref, kv_ref, [now[0:2], now[2:4]])
    prompt_planes(idx_ref, k, now, before, y_rows, qs_ref, sp_in, sp_ref, kv_ref)
    token_ref[...] = jnp.zeros((8, 128), F32)
    wait()


def ext_last_body(idx_ref, qx_ref, fa, fac, fb, fbc, se_in, se_ref, send_ref, kv_ref):
    z, _, plus = around(idx_ref, 4)
    se_ref[...] = se_in[...]
    kv_ref[0, 0:256, :] = fb[0:256, :]
    kv_ref[0, 256:512, :] = fbc[0:256, :]
    kv_ref[0, 512:576, :] = fa[256:320, :]
    kv_ref[0, 576:640, :] = fac[256:320, :]
    ext_plane(z, plus, qx_ref, se_ref, kv_ref.at[0])
    part = se_ref[448:896, :]
    total = part[:, HD:2 * HD]
    level = part[:, :HD] * C1 + jnp.log2(total)
    hi = level.astype(BF)
    rest = level - hi.astype(F32)
    mid = rest.astype(BF)
    low = (rest - mid.astype(F32)).astype(BF)
    lane = lax.broadcasted_iota(jnp.int32, (448, HD), 1)
    stats = jnp.where(
        lane == 0, hi.astype(F32), jnp.where(lane == 1, mid.astype(F32), low.astype(F32))
    )
    send_ref[:, :HD] = (part[:, 2 * HD:] / total).astype(BF)
    send_ref[:, HD:] = stats.astype(BF)


def prompt4_body(idx_ref, table_ref, qs_ref, *refs):
    now, before = refs[:4], refs[4:8]
    sp_in, _, sp_ref, out_ref, kv_ref, sems = refs[8:]
    y_rows = (320, 256)
    wait = page_copies(idx_ref, table_ref, out_ref, sems, step_items(idx_ref, 4, now, y_rows))
    prompt_planes(idx_ref, 4, now, before, y_rows, qs_ref, sp_in, sp_ref, kv_ref)
    wait()


def last_body(
    idx_ref, table_ref, qs_ref, g_ref, gc_ref, ra_ref, rac_ref, rb_ref, rbc_ref, sp_in, se_ref, got_ref, _,
    out_ref, pool_ref, sp_ref, kv_ref, sems,
):
    z, _, _ = position(idx_ref)
    plane = (z + 4) % 8
    shard = shard_at(idx_ref, plane) ^ 2
    wait = page_copies(
        idx_ref, table_ref, pool_ref, sems,
        [
            (shard, ra_ref, 0, None, None), (shard ^ 1, rac_ref, 0, None, None),
            (shard, rb_ref, None, 0, 128), (shard ^ 1, rbc_ref, None, 0, 128),
        ],
    )
    firsts = [g_ref[0:128, :], gc_ref[0:128, :], ra_ref[...], rac_ref[...]]
    sp_ref[0:896, :] = sp_in[0:896, :]
    update(qs_ref, 896, sp_ref, 896, 128, firsts, source=sp_in)
    blocks = [
        ((g_ref, 0), (g_ref, 128)), ((gc_ref, 0), (gc_ref, 128)), ((ra_ref, 0), (rb_ref, 0)), ((rac_ref, 0), (rbc_ref, 0))
    ]
    selected(z, (plane,), qs_ref, sp_ref, kv_ref, [blocks])

    for b in range(2):
        for h in range(HEADS):
            at = slice(b * 896 + h * 128, b * 896 + (h + 1) * 128)
            out_ref[b * 128:(b + 1) * 128, h * HD:(h + 1) * HD] = (
                sp_ref[at, 2 * HD:] / sp_ref[at, HD:2 * HD]
            ).astype(BF)
    for h in range(HEADS):
        at = slice(h * 64, (h + 1) * 64)
        total = se_ref[at, HD:2 * HD]
        level = se_ref[at, :HD] * C1 + jnp.log2(total)
        mine = se_ref[at, 2 * HD:] / total
        got = got_ref[at, :].astype(F32)
        level_y = got[:, HD:HD + 1] + got[:, HD + 1:HD + 2] + got[:, HD + 2:HD + 3]
        top = jnp.maximum(level, level_y)
        wa = jnp.exp2(level - top)
        wb = jnp.exp2(level_y - top)
        out_ref[256:320, h * HD:(h + 1) * HD] = (
            (wa * mine + wb * got[:, :HD]) / (wa + wb)
        ).astype(BF)
    wait()


def body(q_prompt, kv_prompt, q_ext, kv_ext, pool, page_slot_table):
    idx = lax.axis_index("ctx").astype(jnp.int32).reshape(1)
    kvp = kv_prompt.reshape(256, 256)
    kve = kv_ext.reshape(64, 256)
    pages = pool.reshape(6, 128, 256)

    def shift(x, d):
        return lax.ppermute(x, "ctx", [(i, (i + 4 * d) % 32) for i in range(32)])

    def flip_y(x):
        return lax.ppermute(x, "ctx", [(i, i ^ 2) for i in range(32)])

    def flip_c(x):
        return lax.ppermute(x, "ctx", [(i, i ^ 1) for i in range(32)])

    def after(x, token):
        return lax.optimization_barrier((x, token))[0]

    def arr(shape, dtype=BF):
        return jax.ShapeDtypeStruct(shape, dtype)

    def hbm(x):
        return pltpu.with_memory_space_constraint(x, pltpu.HBM)

    x, p = pl.pallas_call(
        prep_body,
        out_shape=(arr((576, 256)), arr((576, 256))),
        in_specs=[SMEM, SMEM, HBM, HBM, HBM, HBM],
        out_specs=(ANY, ANY),
        scratch_shapes=[pltpu.SemaphoreType.DMA((13,))],
        compiler_params=params(),
        name="prep",
    )(idx, hbm(page_slot_table), hbm(pages), hbm(kvp), hbm(kve), hbm(q_ext))

    yp = flip_y(p)
    a1, b1 = shift(x, 1), shift(x, -1)
    xc, yc = flip_c(x), flip_c(yp)
    n1 = (a1, flip_c(a1), b1, flip_c(b1))
    a2 = shift(jnp.concatenate([a1, yp[:320]], axis=0), 1)
    b2 = shift(jnp.concatenate([b1, yp[:320]], axis=0), -1)

    sp_t, se_t, pool_t = arr((1792, 384), F32), arr((896, 384), F32), arr((6, 128, 256))
    token_t = arr((8, 128), F32)
    sems = pltpu.SemaphoreType.DMA((25,))
    kv_t = pltpu.VMEM((2, 640, 256), BF)
    qs, qx, sp, se, new_pool, token = pl.pallas_call(
        first_body,
        out_shape=(arr((1792, 128)), arr((896, 128)), sp_t, se_t, pool_t, token_t),
        in_specs=[SMEM, SMEM] + [VMEM] * 11,
        out_specs=(VMEM,) * 4 + (HBM, VMEM),
        scratch_shapes=[kv_t, sems],
        compiler_params=params(),
        cost_estimate=cost(2e9, 3e6, 4e6),
        name="step1",
    )(idx, page_slot_table, q_prompt, q_ext, x, xc, yp, yc, *n1, pages)

    def step(k, now, before, sp, se, new_pool):
        return pl.pallas_call(
            lambda *refs: step_body(k, *refs),
            out_shape=(sp_t, se_t, pool_t, token_t),
            in_specs=[SMEM, SMEM] + [VMEM] * 12 + [HBM],
            out_specs=(VMEM, VMEM, HBM, VMEM),
            input_output_aliases={12: 0, 13: 1, 14: 2},
            scratch_shapes=[kv_t, sems],
            compiler_params=params(),
            cost_estimate=cost(2e9, 3e6, 8e6),
            name=f"step{k}",
        )(idx, page_slot_table, qs, qx, *now, *before, sp, se, new_pool)

    a2, b2 = after(a2, token), after(b2, token)
    a3, b3 = shift(a2, 1), shift(b2, -1)
    n2 = (a2, flip_c(a2), b2, flip_c(b2))
    sp, se, new_pool, token = step(2, n2, n1, sp, se, new_pool)
    a3, b3 = after(a3, token), after(b3, token)
    a4 = shift(a3[256:896], 1)
    b4 = shift(jnp.concatenate([b3[0:256], b3[576:896]], axis=0), -1)
    n3 = (a3, flip_c(a3), b3, flip_c(b3))
    sp, se, new_pool, token = step(3, n3, n2, sp, se, new_pool)
    a4, b4 = after(a4, token), after(b4, token)
    a5 = shift(a4[320:448], 1)
    b5 = shift(b4[384:576], -1)
    n4 = (a4, flip_c(a4), b4, flip_c(b4))
    se, send = pl.pallas_call(
        ext_last_body,
        out_shape=(se_t, arr((448, 256))),
        in_specs=[SMEM] + [VMEM] * 6,
        out_specs=(VMEM, VMEM),
        input_output_aliases={6: 0},
        scratch_shapes=[kv_t],
        compiler_params=params(),
        cost_estimate=cost(3e8, 6e5, 3e6),
        name="ext4",
    )(idx, qx, *n4, se)
    got = flip_y(send)
    sp, new_pool = pl.pallas_call(
        prompt4_body,
        out_shape=(sp_t, pool_t),
        in_specs=[SMEM, SMEM] + [VMEM] * 10 + [HBM],
        out_specs=(VMEM, HBM),
        input_output_aliases={11: 0, 12: 1},
        scratch_shapes=[kv_t, sems],
        compiler_params=params(),
        cost_estimate=cost(2e9, 2e6, 6e6),
        name="prompt4",
    )(idx, page_slot_table, qs, *n4, *n3, sp, new_pool)
    local_context, new_pool = pl.pallas_call(
        last_body,
        out_shape=(arr((320, 896)), pool_t),
        in_specs=[SMEM, SMEM] + [VMEM] * 10 + [HBM],
        out_specs=(VMEM, HBM),
        input_output_aliases={12: 1},
        scratch_shapes=[pltpu.VMEM((1792, 384), F32), kv_t, sems],
        compiler_params=params(),
        cost_estimate=cost(5e8, 1e6, 4e6),
        name="last",
    )(idx, page_slot_table, qs, a4, n4[1], a5, flip_c(a5), b5, flip_c(b5), sp, se, got, new_pool)
    context = lax.all_to_all(local_context, "tp", split_axis=0, concat_axis=1, tiled=True)
    return context, new_pool.reshape(6, 128, 1, 256)


def solution(mesh):
    in_specs = (
        P("ctx", "tp"),
        P("ctx", "tp", None),
        P("ctx", "tp"),
        P("ctx", "tp", None),
        P("ctx", None, "tp", None),
        P(),
    )
    out_specs = (P(("ctx", "tp"), None), P("ctx", None, "tp", None))
    return jax.shard_map(body, mesh=mesh, in_specs=in_specs, out_specs=out_specs, check_vma=False)
```

```python
import jax
import jax.numpy as jnp
from jax import lax
from jax.experimental import pallas as pl
from jax.experimental.pallas import tpu as pltpu
from jax.sharding import PartitionSpec as P

HEADS = 7
HD = 128
NEG = -1e30
C1 = 1.4426950408889634 * HD ** -0.5
F32 = jnp.float32
BF = jnp.bfloat16

VMEM = pl.BlockSpec(memory_space=pltpu.VMEM)
SMEM = pl.BlockSpec(memory_space=pltpu.SMEM)
ANY = pl.BlockSpec(memory_space=pl.ANY)
HBM = pl.BlockSpec(memory_space=pltpu.HBM)


def params():
    return pltpu.CompilerParams(vmem_limit_bytes=20 << 20)


def cost(flops, elems, nbytes):
    return pl.CostEstimate(flops=int(flops), transcendentals=int(elems), bytes_accessed=int(nbytes))


def update(q_ref, q0, state, rows, chunk, blocks, fix=None, source=None):
    source = state if source is None else source
    kv = blocks[0] if len(blocks) == 1 else jnp.concatenate(blocks, axis=0)
    keys = kv[:, :HD]
    values = jnp.concatenate([jnp.ones((kv.shape[0], HD), BF), kv[:, HD:]], axis=1)
    for r in range(0, rows, chunk):
        at = pl.ds(q0 + r, chunk)
        s = lax.dot_general(
            q_ref[at, :], keys, (((1,), (1,)), ((), ())), preferred_element_type=F32
        )
        if fix is not None:
            s = fix(s, r)
        m_old = source[at, :HD]
        m_new = jnp.maximum(m_old, jnp.max(s, axis=1, keepdims=True))
        p = jnp.exp2((s - jnp.concatenate([m_new] * (s.shape[1] // HD), axis=1)) * C1).astype(BF)
        alpha = jnp.exp2((m_old - m_new) * C1)
        pv = lax.dot_general(p, values, (((1,), (0,)), ((), ())), preferred_element_type=F32)
        state[at, :HD] = m_new
        state[at, HD:] = source[at, HD:] * jnp.concatenate([alpha, alpha], axis=1) + pv


def position(idx_ref):
    i = idx_ref[0]
    return i // 4, (i // 2) % 2, i % 2


def prep_body(idx_ref, table_ref, pool_ref, kvp_ref, kve_ref, qe_ref, x_ref, p_ref, sems):
    base = idx_ref[0] * 6

    def scan(j, found):
        n, a, b = found
        local = table_ref[j] - base
        inside = (local >= 0) & (local < 6)
        a = jnp.where(inside & (n == 0), local, a)
        b = jnp.where(inside & (n == 1), local, b)
        return n + inside.astype(jnp.int32), a, b

    zero = jnp.int32(0)
    early = [
        pltpu.make_async_copy(kvp_ref, x_ref.at[256:512], sems.at[0]),
        pltpu.make_async_copy(kve_ref, x_ref.at[512:576], sems.at[1]),
        pltpu.make_async_copy(kvp_ref, p_ref.at[0:256], sems.at[2]),
        pltpu.make_async_copy(kve_ref, p_ref.at[256:320], sems.at[3]),
    ]
    for h in range(HEADS):
        to = p_ref.at[320 + h // 2 * 64:384 + h // 2 * 64, h % 2 * HD:h % 2 * HD + HD]
        early.append(pltpu.make_async_copy(qe_ref.at[:, h * HD:(h + 1) * HD], to, sems.at[6 + h]))
    for copy in early:
        copy.start()
    found = (zero, zero, zero)
    for j in range(64):
        found = scan(j, found)
    _, a, b = found
    late = [
        pltpu.make_async_copy(pool_ref.at[a], x_ref.at[0:128], sems.at[4]),
        pltpu.make_async_copy(pool_ref.at[b], x_ref.at[128:256], sems.at[5]),
    ]
    for copy in late:
        copy.start()
    for copy in early + late:
        copy.wait()


def page_copies(idx_ref, table_ref, pool_ref, sems, items):
    base = idx_ref[0] * 6
    waits = []

    def add(entry, ref, row, count, to):
        local = table_ref[entry] - base
        go = (local >= 0) & (local < 6)
        sem = sems.at[len(waits)]

        def copy():
            return pltpu.make_async_copy(
                ref.at[row:row + count], pool_ref.at[local, pl.ds(to, count)], sem
            )

        @pl.when(go)
        def _():
            copy().start()

        waits.append((go, copy))

    for shard, ref, front, back, ext in items:
        if front is not None:
            add(80 + shard, ref, front, 128, 0)
        if back is not None:
            add(143 - shard, ref, back, 128, 0)
        if ext is not None:
            add(64 + shard // 2, ref, ext, 64, pl.multiple_of(shard % 2 * 64, 64))

    def wait():
        for go, copy in waits:
            @pl.when(go)
            def _(copy=copy):
                copy().wait()

    return wait


def shard_at(idx_ref, plane):
    return 4 * plane + idx_ref[0] % 4


def ext_plane(z, plane, qx_ref, se_ref, kv):
    bias = jnp.full((1, 128), jnp.where(plane < z, 0.0, NEG), F32)

    def fix(s, _):
        return jnp.concatenate([s[:, :512], s[:, 512:] + bias], axis=1)

    update(qx_ref, 0, se_ref, 896, 448, [kv[...]], fix)


def ext_planes(z, minus, plus, qx_ref, se_ref, kv_ref, parts):
    for i, (r, rc) in enumerate(parts):
        kv_ref[i, 0:256, :] = r[0:256, :]
        kv_ref[i, 256:512, :] = rc[0:256, :]
        kv_ref[i, 512:576, :] = r[512:576, :]
        kv_ref[i, 576:640, :] = rc[512:576, :]

    def one(i, carry):
        ext_plane(z, jnp.where(i == 0, minus, plus), qx_ref, se_ref, kv_ref.at[i])
        return carry

    lax.fori_loop(0, 2, one, 0)


def first_body(
    idx_ref, table_ref, qp_ref, qe_ref, x_ref, xc_ref, y_ref, yc_ref, a_ref, ac_ref, b_ref, bc_ref, pool_ref,
    qs_ref, qx_ref, sp_ref, se_ref, out_ref, token_ref, kv_ref, sems,
):
    z, y, c = position(idx_ref)
    j = 2 * y + c
    whole = pltpu.make_async_copy(pool_ref, out_ref, sems.at[24])
    whole.start()
    for h in range(HEADS):
        cols = slice(h * HD, (h + 1) * HD)
        qs_ref[h * 128:(h + 1) * 128, :] = qp_ref[0:128, cols]
        qs_ref[896 + h * 128:896 + (h + 1) * 128, :] = qp_ref[128:256, cols]
        qx_ref[h * 64:(h + 1) * 64, :] = qe_ref[:, cols]
        qx_ref[448 + h * 64:448 + (h + 1) * 64, :] = y_ref[320 + h // 2 * 64:384 + h // 2 * 64, h % 2 * HD:h % 2 * HD + HD]
    for state in (sp_ref, se_ref):
        state[:, :HD] = jnp.full((state.shape[0], HD), NEG, F32)
        state[:, HD:] = jnp.zeros((state.shape[0], 2 * HD), F32)
    whole.wait()
    minus = (z + 7) % 8
    plus = (z + 1) % 8
    own = idx_ref[0]
    am, bm = shard_at(idx_ref, minus), shard_at(idx_ref, plus)
    wait = page_copies(
        idx_ref, table_ref, out_ref, sems,
        [
            (own, x_ref, 256, 384, 512), (own ^ 1, xc_ref, 256, 384, 512),
            (own ^ 2, y_ref, 0, 128, 256), (own ^ 3, yc_ref, 0, 128, 256),
            (am, a_ref, 256, 384, 512), (am ^ 1, ac_ref, 256, 384, 512),
            (bm, b_ref, 256, 384, 512), (bm ^ 1, bc_ref, 256, 384, 512),
        ],
    )

    def shown(seen, width):
        return jnp.full((1, width), jnp.where(seen, 0.0, NEG), F32)

    rows = lax.broadcasted_iota(jnp.int32, (128, 128), 0)
    lanes = lax.broadcasted_iota(jnp.int32, (128, 128), 1)
    causal = jnp.where(rows >= lanes, 0.0, NEG).astype(F32)
    others = (j ^ 1, j ^ 2, j ^ 3)
    front = jnp.concatenate([shown(o < j, 128) for o in others], axis=1)
    back = jnp.concatenate([shown(o > j, 128) for o in others], axis=1)

    def fix_front(s, r):
        return jnp.concatenate([s[:, :128] + causal, s[:, 128:] + front], axis=1)

    def fix_back(s, r):
        return jnp.concatenate([s[:, :512], s[:, 512:640] + causal, s[:, 640:] + back], axis=1)

    firsts = [x_ref[256:384, :], xc_ref[256:384, :], y_ref[0:128, :], yc_ref[0:128, :]]
    seconds = [x_ref[384:512, :], xc_ref[384:512, :], y_ref[128:256, :], yc_ref[128:256, :]]
    update(qs_ref, 0, sp_ref, 896, 128, firsts, fix_front)
    update(qs_ref, 896, sp_ref, 896, 128, firsts + seconds, fix_back)

    tokens = lax.broadcasted_iota(jnp.int32, (448, 128), 0) % 64
    slots = lax.broadcasted_iota(jnp.int32, (448, 128), 1)
    mine = jnp.where(
        slots < 64,
        jnp.where(tokens >= slots, 0.0, NEG).astype(F32),
        jnp.full((448, 128), jnp.where(c == 1, 0.0, NEG), F32),
    )
    mate = shown(y == 0, 128)

    def fix_ext(s, r):
        tail = s[:, 512:] + (mine if r == 0 else mate)
        return jnp.concatenate([s[:, :512], tail], axis=1)

    update(
        qx_ref, 0, se_ref, 896, 448,
        [x_ref[0:256, :], xc_ref[0:256, :], x_ref[512:576, :], xc_ref[512:576, :]], fix_ext,
    )
    ext_planes(z, minus, plus, qx_ref, se_ref, kv_ref, [(a_ref, ac_ref), (b_ref, bc_ref)])
    token_ref[...] = jnp.zeros((8, 128), F32)
    wait()


def selected(z, planes, qs_ref, sp_ref, kv_ref, parts):
    for i, (plane, blocks) in enumerate(zip(planes, parts)):
        for side in range(2):
            @pl.when((plane > z) == (side == 1))
            def _(i=i, side=side, blocks=blocks):
                for n, block in enumerate(blocks):
                    ref, row = block[side]
                    kv_ref[i, n * 128:(n + 1) * 128, :] = ref[row:row + 128, :]

    def one(i, carry):
        plane = planes[0] if len(planes) == 1 else jnp.where(i == 0, planes[0], planes[1])
        q0 = pl.multiple_of(jnp.where(plane > z, 896, 0), 128)
        update(qs_ref, q0, sp_ref, 896, 128, [kv_ref[i, 0:512, :]])
        return carry

    if len(planes) == 1:
        one(0, 0)
    else:
        lax.fori_loop(0, 2, one, 0)


def around(idx_ref, k):
    z, _, _ = position(idx_ref)
    return z, (z + 8 - k) % 8, (z + k) % 8


def prompt_planes(idx_ref, k, now, before, y_rows, qs_ref, sp_in, sp_ref, kv_ref):
    z, minus, plus = around(idx_ref, k - 1)
    sp_ref[0:896, :] = sp_in[0:896, :]
    parts = []
    for i in range(2):
        shards = [(before[2 * i], 256), (before[2 * i + 1], 256), (now[2 * i], y_rows[i]), (now[2 * i + 1], y_rows[i])]
        parts.append([((ref, row), (ref, row + 128)) for ref, row in shards])
    blocks = [(now[i], y_rows[i // 2]) for i in range(4)]
    blocks += [(now[0], 0), (now[1], 0)] if k == 4 else [(ref, 256) for ref in now]
    if k == 2:
        blocks += [(ref, 256) for ref in before]
    fronts = [ref[row:row + 128, :] for ref, row in blocks]
    update(qs_ref, 896, sp_ref, 896, 128, fronts, source=sp_in)
    selected(z, (minus, plus), qs_ref, sp_ref, kv_ref, parts)


def step_items(idx_ref, k, now, y_rows):
    _, minus, plus = around(idx_ref, k)
    _, minus1, plus1 = around(idx_ref, k - 1)
    am, bm = shard_at(idx_ref, minus), shard_at(idx_ref, plus)
    am1, bm1 = shard_at(idx_ref, minus1) ^ 2, shard_at(idx_ref, plus1) ^ 2
    fa, fac, fb, fbc = now
    if k < 4:
        items = [
            (am, fa, 256, 384, 512), (am ^ 1, fac, 256, 384, 512),
            (bm, fb, 256, 384, 512), (bm ^ 1, fbc, 256, 384, 512),
        ]
    else:
        items = [(am, fa, 0, 128, 256), (am ^ 1, fac, 0, 128, 256)]
    ya, yb = y_rows
    return items + [
        (am1, fa, ya, ya + 128, ya + 256), (am1 ^ 1, fac, ya, ya + 128, ya + 256),
        (bm1, fb, yb, yb + 128, yb + 256), (bm1 ^ 1, fbc, yb, yb + 128, yb + 256),
    ]


def step_body(k, *refs):
    idx_ref, table_ref, qs_ref, qx_ref = refs[:4]
    now, before = refs[4:8], refs[8:12]
    sp_in, se_in, _, sp_ref, se_ref, out_ref, token_ref, kv_ref, sems = refs[12:]
    y_rows = (576, 576)
    wait = page_copies(idx_ref, table_ref, out_ref, sems, step_items(idx_ref, k, now, y_rows))
    z, minus, plus = around(idx_ref, k)
    se_ref[...] = se_in[...]
    ext_planes(z, minus, plus, qx_ref, se_ref, kv_ref, [now[0:2], now[2:4]])
    prompt_planes(idx_ref, k, now, before, y_rows, qs_ref, sp_in, sp_ref, kv_ref)
    token_ref[...] = jnp.zeros((8, 128), F32)
    wait()


def ext_last_body(idx_ref, qx_ref, fa, fac, fb, fbc, se_in, se_ref, send_ref, kv_ref):
    z, _, plus = around(idx_ref, 4)
    se_ref[...] = se_in[...]
    kv_ref[0, 0:256, :] = fb[0:256, :]
    kv_ref[0, 256:512, :] = fbc[0:256, :]
    kv_ref[0, 512:576, :] = fa[256:320, :]
    kv_ref[0, 576:640, :] = fac[256:320, :]
    ext_plane(z, plus, qx_ref, se_ref, kv_ref.at[0])
    part = se_ref[448:896, :]
    total = part[:, HD:2 * HD]
    level = part[:, :HD] * C1 + jnp.log2(total)
    hi = level.astype(BF)
    rest = level - hi.astype(F32)
    mid = rest.astype(BF)
    low = (rest - mid.astype(F32)).astype(BF)
    lane = lax.broadcasted_iota(jnp.int32, (448, HD), 1)
    stats = jnp.where(
        lane == 0, hi.astype(F32), jnp.where(lane == 1, mid.astype(F32), low.astype(F32))
    )
    send_ref[:, :HD] = (part[:, 2 * HD:] / total).astype(BF)
    send_ref[:, HD:] = stats.astype(BF)


def prompt4_body(idx_ref, table_ref, qs_ref, *refs):
    now, before = refs[:4], refs[4:8]
    sp_in, _, sp_ref, out_ref, kv_ref, sems = refs[8:]
    y_rows = (320, 256)
    wait = page_copies(idx_ref, table_ref, out_ref, sems, step_items(idx_ref, 4, now, y_rows))
    prompt_planes(idx_ref, 4, now, before, y_rows, qs_ref, sp_in, sp_ref, kv_ref)
    wait()


def last_body(
    idx_ref, table_ref, qs_ref, g_ref, gc_ref, ra_ref, rac_ref, rb_ref, rbc_ref, sp_in, se_ref, got_ref, _,
    out_ref, pool_ref, sp_ref, kv_ref, sems,
):
    z, _, _ = position(idx_ref)
    plane = (z + 4) % 8
    shard = shard_at(idx_ref, plane) ^ 2
    wait = page_copies(
        idx_ref, table_ref, pool_ref, sems,
        [
            (shard, ra_ref, 0, None, None), (shard ^ 1, rac_ref, 0, None, None),
            (shard, rb_ref, None, 0, 128), (shard ^ 1, rbc_ref, None, 0, 128),
        ],
    )
    firsts = [ra_ref[...], rac_ref[...]]
    sp_ref[0:896, :] = sp_in[0:896, :]
    update(qs_ref, 896, sp_ref, 896, 128, firsts, source=sp_in)
    blocks = [
        ((g_ref, 0), (g_ref, 128)), ((gc_ref, 0), (gc_ref, 128)), ((ra_ref, 0), (rb_ref, 0)), ((rac_ref, 0), (rbc_ref, 0))
    ]
    selected(z, (plane,), qs_ref, sp_ref, kv_ref, [blocks])

    for b in range(2):
        for h in range(HEADS):
            at = slice(b * 896 + h * 128, b * 896 + (h + 1) * 128)
            out_ref[b * 128:(b + 1) * 128, h * HD:(h + 1) * HD] = (
                sp_ref[at, 2 * HD:] / sp_ref[at, HD:2 * HD]
            ).astype(BF)
    for h in range(HEADS):
        at = slice(h * 64, (h + 1) * 64)
        total = se_ref[at, HD:2 * HD]
        level = se_ref[at, :HD] * C1 + jnp.log2(total)
        mine = se_ref[at, 2 * HD:] / total
        got = got_ref[at, :].astype(F32)
        level_y = got[:, HD:HD + 1] + got[:, HD + 1:HD + 2] + got[:, HD + 2:HD + 3]
        top = jnp.maximum(level, level_y)
        wa = jnp.exp2(level - top)
        wb = jnp.exp2(level_y - top)
        out_ref[256:320, h * HD:(h + 1) * HD] = (
            (wa * mine + wb * got[:, :HD]) / (wa + wb)
        ).astype(BF)
    wait()


def body(q_prompt, kv_prompt, q_ext, kv_ext, pool, page_slot_table):
    idx = lax.axis_index("ctx").astype(jnp.int32).reshape(1)
    kvp = kv_prompt.reshape(256, 256)
    kve = kv_ext.reshape(64, 256)
    pages = pool.reshape(6, 128, 256)

    def shift(x, d):
        return lax.ppermute(x, "ctx", [(i, (i + 4 * d) % 32) for i in range(32)])

    def flip_y(x):
        return lax.ppermute(x, "ctx", [(i, i ^ 2) for i in range(32)])

    def flip_c(x):
        return lax.ppermute(x, "ctx", [(i, i ^ 1) for i in range(32)])

    def after(x, token):
        return lax.optimization_barrier((x, token))[0]

    def arr(shape, dtype=BF):
        return jax.ShapeDtypeStruct(shape, dtype)

    def hbm(x):
        return pltpu.with_memory_space_constraint(x, pltpu.HBM)

    x, p = pl.pallas_call(
        prep_body,
        out_shape=(arr((576, 256)), arr((576, 256))),
        in_specs=[SMEM, SMEM, HBM, HBM, HBM, HBM],
        out_specs=(ANY, ANY),
        scratch_shapes=[pltpu.SemaphoreType.DMA((13,))],
        compiler_params=params(),
        name="prep",
    )(idx, hbm(page_slot_table), hbm(pages), hbm(kvp), hbm(kve), hbm(q_ext))

    yp = flip_y(p)
    a1, b1 = shift(x, 1), shift(x, -1)
    xc, yc = flip_c(x), flip_c(yp)
    n1 = (a1, flip_c(a1), b1, flip_c(b1))
    a2 = shift(jnp.concatenate([a1, yp[:320]], axis=0), 1)
    b2 = shift(jnp.concatenate([b1, yp[:320]], axis=0), -1)

    sp_t, se_t, pool_t = arr((1792, 384), F32), arr((896, 384), F32), arr((6, 128, 256))
    token_t = arr((8, 128), F32)
    sems = pltpu.SemaphoreType.DMA((25,))
    kv_t = pltpu.VMEM((2, 640, 256), BF)
    qs, qx, sp, se, new_pool, token = pl.pallas_call(
        first_body,
        out_shape=(arr((1792, 128)), arr((896, 128)), sp_t, se_t, pool_t, token_t),
        in_specs=[SMEM, SMEM] + [VMEM] * 11,
        out_specs=(VMEM,) * 4 + (HBM, VMEM),
        scratch_shapes=[kv_t, sems],
        compiler_params=params(),
        cost_estimate=cost(2e9, 3e6, 4e6),
        name="step1",
    )(idx, page_slot_table, q_prompt, q_ext, x, xc, yp, yc, *n1, pages)

    def step(k, now, before, sp, se, new_pool):
        return pl.pallas_call(
            lambda *refs: step_body(k, *refs),
            out_shape=(sp_t, se_t, pool_t, token_t),
            in_specs=[SMEM, SMEM] + [VMEM] * 12 + [HBM],
            out_specs=(VMEM, VMEM, HBM, VMEM),
            input_output_aliases={12: 0, 13: 1, 14: 2},
            scratch_shapes=[kv_t, sems],
            compiler_params=params(),
            cost_estimate=cost(2e9, 3e6, 8e6),
            name=f"step{k}",
        )(idx, page_slot_table, qs, qx, *now, *before, sp, se, new_pool)

    a2, b2 = after(a2, token), after(b2, token)
    a3, b3 = shift(a2, 1), shift(b2, -1)
    n2 = (a2, flip_c(a2), b2, flip_c(b2))
    sp, se, new_pool, token = step(2, n2, n1, sp, se, new_pool)
    a3, b3 = after(a3, token), after(b3, token)
    a4 = shift(a3[256:896], 1)
    b4 = shift(jnp.concatenate([b3[0:256], b3[576:896]], axis=0), -1)
    n3 = (a3, flip_c(a3), b3, flip_c(b3))
    sp, se, new_pool, token = step(3, n3, n2, sp, se, new_pool)
    a4, b4 = after(a4, token), after(b4, token)
    a5 = shift(a4[320:448], 1)
    b5 = shift(b4[384:576], -1)
    n4 = (a4, flip_c(a4), b4, flip_c(b4))
    se, send = pl.pallas_call(
        ext_last_body,
        out_shape=(se_t, arr((448, 256))),
        in_specs=[SMEM] + [VMEM] * 6,
        out_specs=(VMEM, VMEM),
        input_output_aliases={6: 0},
        scratch_shapes=[kv_t],
        compiler_params=params(),
        cost_estimate=cost(3e8, 6e5, 3e6),
        name="ext4",
    )(idx, qx, *n4, se)
    got = flip_y(send)
    sp, new_pool = pl.pallas_call(
        prompt4_body,
        out_shape=(sp_t, pool_t),
        in_specs=[SMEM, SMEM] + [VMEM] * 10 + [HBM],
        out_specs=(VMEM, HBM),
        input_output_aliases={11: 0, 12: 1},
        scratch_shapes=[kv_t, sems],
        compiler_params=params(),
        cost_estimate=cost(2e9, 2e6, 6e6),
        name="prompt4",
    )(idx, page_slot_table, qs, *n4, *n3, sp, new_pool)
    local_context, new_pool = pl.pallas_call(
        last_body,
        out_shape=(arr((320, 896)), pool_t),
        in_specs=[SMEM, SMEM] + [VMEM] * 10 + [HBM],
        out_specs=(VMEM, HBM),
        input_output_aliases={12: 1},
        scratch_shapes=[pltpu.VMEM((1792, 384), F32), kv_t, sems],
        compiler_params=params(),
        cost_estimate=cost(5e8, 1e6, 4e6),
        name="last",
    )(idx, page_slot_table, qs, a4, n4[1], a5, flip_c(a5), b5, flip_c(b5), sp, se, got, new_pool)
    context = lax.all_to_all(local_context, "tp", split_axis=0, concat_axis=1, tiled=True)
    return context, new_pool.reshape(6, 128, 1, 256)


def solution(mesh):
    in_specs = (
        P("ctx", "tp"),
        P("ctx", "tp", None),
        P("ctx", "tp"),
        P("ctx", "tp", None),
        P("ctx", None, "tp", None),
        P(),
    )
    out_specs = (P(("ctx", "tp"), None), P("ctx", None, "tp", None))
    return jax.shard_map(body, mesh=mesh, in_specs=in_specs, out_specs=out_specs, check_vma=False)
```
